256 devices in a mesh: order: 16 (over x_hi, z), blk: 16 (over y, x_lo, core).
Axes of the slice: x: 4 (x_hi: 2, x_lo: 2; x = x_hi * 2 + x_lo), y: 4, z: 8, core: 2. Of those that a mesh axis runs over, the one named last changes fastest.
Arguments:
- fourier_cycles: float32 [32, 512, 128], P('order', 'blk'), parts along dimension 0, may hold values from -6 to 6
- legendre: float32 [32, 512, 12288], P('order', 'blk'), parts along dimension 0, may hold values from -0.25 to 0.25
- cycle_weight: float32 [512], P('blk'), may hold values from 0.5 to 2
- matched_filter_weights: float32 [12288, 8, 8], P('blk'), may hold values from -2 to 2
- cluster_cycles: int32 [32, 64], P('order'), parts along dimension 0, may hold values from 0 to 511
- cluster_flux: float32 [32, 64, 128], P('order'), parts along dimension 0, may hold values from -18 to 18
- order_per_slot: int32 [32], P('order'), parts along dimension 0, may hold values from 0 to 6143
Outputs:
- synthesized: float32 [32, 512, 128], P('order', 'blk'), parts along dimension 0
The draws below stay inside these ranges and needn't reach their ends.
There are 16 independent parts, one for each index of `order`. The reference program is written for one: setup_inputs(seed, part) draws one part's arguments, and reference() takes and returns one part's arrays. A program takes and returns all parts, laid end to end along the dimension named above; an argument that names none is the same for every part. Nothing has to cross between parts.
Inputs may be any that keep to these rules, and one draw needn't show every extreme that they name: `cluster_cycles`: cycle indices; several clusters may share a cycle, and their coefficients add. `order_per_slot`: order of each slot; degrees below it carry no coefficients.
All inputs are finite; a program needn't handle non-finite values.
Results may differ from the reference program's by a relative error of at most 0.00011.
Values sent between devices are 32-bit elements; how exact they have to be, the bound alone decides.
A program may use at most 128 MiB of HBM per device.

```python
import math
import jax
import jax.numpy as jnp
from jax import lax

L = 12288
F = 8
S = 8
SIMS = 8
M = 2
CLUSTERS = 64
R = 512


def with_ends(array, own_key, low, high):
    dims = array.shape
    index_at = [jax.random.randint(jax.random.fold_in(own_key, axis), (), 0, dims[axis]) for axis in range(len(dims))]
    array = array.at[tuple(index_at)].set(low)
    longest = dims.index(max(dims))
    index_at[longest] = (index_at[longest] + 1) % dims[longest]
    return array.at[tuple(index_at)].set(high)


def level_of(own_key, shape, shards, low, top_value):
    gain = 1.0
    for position, shards_of in shards:
        draws = jax.random.uniform(jax.random.fold_in(jax.random.fold_in(own_key, 6), position), (shards_of,), jnp.float32, low / len(shards), top_value / len(shards))
        gain = gain * jnp.repeat(jnp.exp(draws), shape[position] // shards_of).reshape((-1,) + (1,) * (len(shape) - 1 - position))
    return gain


def normal_values(rng, extent, deviation, bound, split=(), kind=jnp.bfloat16):
    array = jax.random.normal(rng, extent, jnp.float32) * deviation
    if len(split) > 0:
        array = level_of(rng, extent, split, -0.22, 0.18) * array
    return jnp.clip(array, min=-bound, max=bound).astype(kind)


def setup_inputs(seed: int = 0, part: int = 0) -> dict:
    arg_keys = jax.random.split(jax.random.key(seed), 8)
    part_keys = jax.random.split(jax.random.fold_in(arg_keys[7], part), 8)
    fourier_cycles = normal_values(part_keys[0], (M, R, 2 * F * SIMS), 1.0, 6.0, ((1, 16),), jnp.float32)
    legendre = normal_values(part_keys[1], (M, R, L), R ** -0.5, 0.25, ((1, 16),), jnp.float32)
    cycle_weight = jnp.clip(jnp.exp(math.log(2.0) - 1.3862944 * jax.random.uniform(arg_keys[2], (R,), jnp.float32) ** level_of(arg_keys[2], (R,), ((0, 16),), -0.2, 0.2)), 0.5, 2.0)
    matched_filter_weights = normal_values(arg_keys[3], (L, S, F), F ** -0.5, 2.0, ((0, 16),), jnp.float32)
    cluster_cycles = with_ends(jax.random.randint(part_keys[4], (M, CLUSTERS), 0, R), jax.random.fold_in(part_keys[4], 1), 0, R - 1).astype(jnp.int32)
    cluster_flux = normal_values(part_keys[5], (M, CLUSTERS, 2 * F * SIMS), 3.0, 18.0, (), jnp.float32)
    order_per_slot = jax.random.randint(part_keys[6], (M,), 0, L // 2).astype(jnp.int32)
    return {"fourier_cycles": fourier_cycles, "legendre": legendre, "cycle_weight": cycle_weight, "matched_filter_weights": matched_filter_weights, "cluster_cycles": cluster_cycles, "cluster_flux": cluster_flux, "order_per_slot": order_per_slot}


highest_degree = lax.Precision.HIGHEST

def inject(fourier_cycles, cycle_weight, cluster_cycles, cluster_flux, cycle_ids):
    cycle_hits = (cycle_ids[None, :, None] == cluster_cycles[:, None, :]).astype(jnp.float32)
    added = jnp.einsum('krj,kjc->krc', cycle_hits, cluster_flux, precision=highest_degree)
    return cycle_weight[None, :, None] * (fourier_cycles + added)

def apply_filter(harmonics, matched_filter_weights, degrees, order_per_slot):
    kept_mask = (degrees[:, None] >= order_per_slot[None, :]).astype(jnp.float32)
    blocks = harmonics.shape[0]
    masked_values = (harmonics * kept_mask[:, :, None]).reshape(blocks, M, 2, F, SIMS)
    matched_output = jnp.einsum('dvr,dotrq->dotvq', matched_filter_weights, masked_values, precision=highest_degree)
    squares = lax.optimization_barrier(jnp.sum(matched_filter_weights * matched_filter_weights, axis=2))
    weights = kept_mask * (2.0 * degrees.astype(jnp.float32) + 1.0)[:, None]
    response = jnp.einsum('lk,ls->ks', weights, squares, precision=highest_degree)
    return (matched_output, response)

def reference(fourier_cycles, legendre, cycle_weight, matched_filter_weights, cluster_cycles, cluster_flux, order_per_slot):
    cycle_ids = jnp.arange(fourier_cycles.shape[1], dtype=jnp.int32)
    injected = inject(fourier_cycles, cycle_weight, cluster_cycles, cluster_flux, cycle_ids)
    harmonics = jnp.einsum('krl,krc->lkc', legendre, injected, precision=highest_degree)
    degrees = jnp.arange(L, dtype=jnp.int32)
    matched_output, response = apply_filter(harmonics, matched_filter_weights, degrees, order_per_slot)
    scaled = matched_output * (L / jnp.sqrt(response))[None, :, None, :, None]
    scaled = scaled.reshape(L, M, 2 * S * SIMS)
    return jnp.einsum('krl,lkc->krc', legendre, scaled, precision=highest_degree)
```

```python
import functools

import jax
import jax.numpy as jnp
from jax import lax
from jax.experimental import pallas as pl
from jax.experimental.pallas import tpu as pltpu
from jax.sharding import PartitionSpec as P

L = 12288
F = 8
S = 8
SIMS = 8
M = 2
Y, X, CORES = 4, 2, 2
CHIPS = Y * X
N = CHIPS * CORES
CHUNKS = 3

MESH = pl.DeviceIdType.MESH
F32 = jnp.float32
BF16 = jnp.bfloat16

STEPS = [(dy, dx, dc) for dy in (1, 3, 2, 0) for dx in (0, 1) for dc in (0, 1) if (dy, dx, dc) != (0, 0, 0)]
CHIP_STEPS = [(dy, dx) for dy, dx, dc in STEPS if dc == 0]


def halves(value):
    high = value.astype(BF16)
    return high, (value - high.astype(F32)).astype(BF16)


def dot(a, b, dims=((1,), (0,))):
    return lax.dot_general(a, b, (dims, ((), ())), preferred_element_type=F32)


def kernel(
    cycles_hbm, legendre_hbm, weight_hbm, filter_hbm, hit_hbm, flux_hbm, order_ref, out_ref,
    own_cycles, own_weight, filters, hits, flux, load_sem,
    injected, injected_t, inj_send, inj_recv, pair_sem,
    responses, resp_send, resp_recv,
    blocks, block_send, block_recv, own_sem,
    high, low, harmonics, matched, total, from_core, core_sem, outgoing, arriving, sum_send, sum_recv,
):
    me = lax.axis_index("blk")
    y, x, core = me // (X * CORES), (me // CORES) % X, me % CORES
    chip = me // CORES
    rows = own_cycles.shape[1]
    half = CHIPS * rows
    degrees = filters.shape[2]
    wide = degrees // CHUNKS

    def chip_at(dy, dx):
        return ((y + dy) % Y) * X + (x + dx) % X

    def at(dy, dx, dc):
        return {"blk": chip_at(dy, dx) * CORES + (core + dc) % CORES}

    barrier = pltpu.get_barrier_semaphore()
    for step in STEPS:
        pl.semaphore_signal(barrier, inc=1, device_id=at(*step), device_id_type=MESH)

    loads = [
        pltpu.make_async_copy(source, target, load_sem.at[i])
        for i, (source, target) in enumerate(
            ((cycles_hbm, own_cycles), (weight_hbm, own_weight), (hit_hbm, hits), (flux_hbm, flux), (filter_hbm, filters))
        )
    ]
    for load in loads:
        load.start()

    own_rows = pl.ds(pl.multiple_of(half + chip * rows, rows), rows)

    def own_copy(j):
        return pltpu.make_async_copy(
            legendre_hbm.at[:, :, pl.ds(pl.multiple_of(me * degrees + j * wide, wide), wide)],
            blocks.at[j, :, own_rows, :],
            own_sem.at[j],
        )

    for j in range(CHUNKS):
        own_copy(j).start()
    for load in loads[:4]:
        load.wait()

    row = lax.broadcasted_iota(jnp.int32, (rows, rows), 0)
    lane = lax.broadcasted_iota(jnp.int32, (rows, rows), 1)
    weight = jnp.sum(jnp.where(row == lane, own_weight[...], 0.0), axis=1, keepdims=True)
    for k in range(M):
        clusters = hits.shape[1]
        cycle = me * rows + lax.broadcasted_iota(jnp.int32, (rows, clusters), 0)
        hit = (cycle == hits[k : k + 1, :]).astype(F32)
        added = lax.dot_general(
            hit, flux[k], (((1,), (0,)), ((), ())), precision=lax.Precision.HIGHEST, preferred_element_type=F32
        )
        injected[k, own_rows, :] = weight * (own_cycles[k] + added)

    loads[4].wait()
    degree = me * degrees + lax.broadcasted_iota(jnp.int32, (1, degrees), 1)
    squares = jnp.sum(filters[...] * filters[...], axis=1)
    scale_of = (lax.broadcasted_iota(jnp.int32, (S, 128), 1) // SIMS) % S == lax.broadcasted_iota(jnp.int32, (S, 128), 0)
    for k in range(M):
        factor = jnp.where(degree >= order_ref[k], 2.0 * degree.astype(F32) + 1.0, 0.0)
        response = jnp.sum(squares * factor, axis=1, keepdims=True)
        responses[me, k : k + 1, :] = jnp.sum(jnp.where(scale_of, response, 0.0), axis=0, keepdims=True)

    pl.semaphore_wait(barrier, N - 1)

    inj_copies = [
        pltpu.make_async_remote_copy(
            src_ref=injected.at[:, own_rows, :],
            dst_ref=injected.at[:, own_rows, :],
            send_sem=inj_send.at[i],
            recv_sem=inj_recv.at[i],
            device_id=at(dy, dx, 0),
            device_id_type=MESH,
        )
        for i, (dy, dx) in enumerate(CHIP_STEPS)
    ]
    for copy in inj_copies:
        copy.start()
    resp_copies = [
        pltpu.make_async_remote_copy(
            src_ref=responses.at[me],
            dst_ref=responses.at[me],
            send_sem=resp_send.at[i],
            recv_sem=resp_recv.at[i],
            device_id=at(*step),
            device_id_type=MESH,
        )
        for i, step in enumerate(STEPS)
    ]
    for copy in resp_copies:
        copy.start()

    def block_copy(j, i):
        dy, dx, dc = STEPS[i]
        there = chip_at(dy, dx) * CORES + (core + dc) % CORES
        return pltpu.make_async_remote_copy(
            src_ref=legendre_hbm.at[:, :, pl.ds(pl.multiple_of(there * degrees + j * wide, wide), wide)],
            dst_ref=blocks.at[j, :, pl.ds(pl.multiple_of((1 - dc) * half + chip * rows, rows), rows), :],
            send_sem=block_send.at[j, i],
            recv_sem=block_recv.at[j, i],
            device_id={"blk": there},
            device_id_type=MESH,
        )

    for j in range(CHUNKS):
        for i in range(N - 1):
            block_copy(j, i).start()

    for copy in inj_copies:
        copy.wait_recv()
    pair = pltpu.make_async_remote_copy(
        src_ref=injected.at[:, pl.ds(half, half), :],
        dst_ref=injected.at[:, pl.ds(0, half), :],
        send_sem=pair_sem.at[0],
        recv_sem=pair_sem.at[1],
        device_id=at(0, 0, 1),
        device_id_type=MESH,
    )
    pair.start()
    pair.wait_recv()
    for k in range(M):
        turned = jnp.transpose(injected[k])
        turned_high, turned_low = halves(turned)
        injected_t[k, 0:128, :] = turned_high
        injected_t[k, 128:256, :] = turned_low

    total[...] = jnp.zeros_like(total)
    core_copy = pltpu.make_async_remote_copy(
        src_ref=total.at[:, pl.ds(0, half), :],
        dst_ref=from_core,
        send_sem=core_sem.at[0],
        recv_sem=core_sem.at[1],
        device_id=at(0, 0, 1),
        device_id_type=MESH,
    )

    def chunk(j, carry):
        own_copy(j).wait()
        for i in range(N - 1):
            block_copy(j, i).wait_recv()
        start = pl.multiple_of(j * wide, wide)
        degree = me * degrees + j * wide + lax.broadcasted_iota(jnp.int32, (1, wide), 1)
        for k in range(M):
            block_high, block_low = halves(blocks[j, k])
            high[k] = block_high
            low[k] = block_low
            first = dot(injected_t[k], high[k])
            second = dot(injected_t[k, 0:128], low[k])
            value = first[0:128] + first[128:256] + second
            harmonics[k] = jnp.where(degree >= order_ref[k], value, 0.0)
            for t in range(wide // 128):
                lanes = pl.ds(t * 128, 128)
                for s in range(S):
                    sums = [None, None]
                    for f in range(F):
                        row = filters[s, f : f + 1, pl.ds(start + t * 128, 128)]
                        for p in range(2):
                            term = row * harmonics[k, pl.ds((p * F + f) * SIMS, SIMS), lanes]
                            sums[p] = term if f == 0 else sums[p] + term
                    for p in range(2):
                        out_high, out_low = halves(sums[p])
                        matched[k, pl.ds((p * S + s) * SIMS, SIMS), lanes] = out_high
                        matched[k, pl.ds(128 + (p * S + s) * SIMS, SIMS), lanes] = out_low
        for part in range(2):
            span = pl.ds(part * half, half)
            for k in range(M):
                both = dot(high[k, span, :], matched[k], ((1,), (1,)))
                third = dot(low[k, span, :], matched[k, 0:128], ((1,), (1,)))
                total[k, span, :] += both[:, 0:128] + both[:, 128:256] + third
            if part == 0:

                @pl.when(j == CHUNKS - 1)
                def _():
                    core_copy.start()

        return carry

    lax.fori_loop(0, CHUNKS, chunk, 0)

    for copy in resp_copies:
        copy.wait_recv()
    scale = L / jnp.sqrt(jnp.sum(responses[...], axis=0))
    core_copy.wait_recv()
    sum_copies = []
    for i, (dy, dx) in enumerate(CHIP_STEPS):
        there = chip_at(dy, dx) * rows
        outgoing[i] = (
            total[:, pl.ds(pl.multiple_of(half + there, rows), rows), :]
            + from_core[:, pl.ds(pl.multiple_of(there, rows), rows), :]
        )
        sum_copies.append(
            pltpu.make_async_remote_copy(
                src_ref=outgoing.at[i],
                dst_ref=arriving.at[i],
                send_sem=sum_send.at[i],
                recv_sem=sum_recv.at[i],
                device_id=at(dy, dx, 0),
                device_id_type=MESH,
            )
        )
    kept = total[:, own_rows, :] + from_core[:, pl.ds(pl.multiple_of(chip * rows, rows), rows), :]
    for copy in sum_copies:
        copy.start()
    for i, copy in enumerate(sum_copies):
        copy.wait_recv()
        kept = kept + arriving[i]
    out_ref[...] = kept * scale[:, None, :]

    for copy in inj_copies + resp_copies + [pair, core_copy] + sum_copies:
        copy.wait_send()
    for j in range(CHUNKS):
        for i in range(N - 1):
            block_copy(j, i).wait_send()


def body(cycles, legendre, weight, filters, hits, flux, order):
    orders, rows, width = cycles.shape
    degrees = filters.shape[0]
    clusters = hits.shape[1]
    wide = degrees // CHUNKS
    everyone = N * rows
    dma = pltpu.SemaphoreType.DMA
    anywhere = pl.BlockSpec(memory_space=pl.ANY)
    return pl.pallas_call(
        kernel,
        out_shape=jax.ShapeDtypeStruct(cycles.shape, F32),
        in_specs=[anywhere] * 6 + [pl.BlockSpec(memory_space=pltpu.SMEM)],
        out_specs=pl.BlockSpec(memory_space=pltpu.VMEM),
        scratch_shapes=[
            pltpu.VMEM((orders, rows, width), F32),
            pltpu.VMEM((1, rows), F32),
            pltpu.VMEM((S, F, degrees), F32),
            pltpu.VMEM((orders, clusters), jnp.int32),
            pltpu.VMEM((orders, clusters, width), F32),
            dma((5,)),
            pltpu.VMEM((orders, everyone, width), F32),
            pltpu.VMEM((orders, 2 * width, everyone), BF16),
            dma((CHIPS - 1,)),
            dma((CHIPS - 1,)),
            dma((2,)),
            pltpu.VMEM((N, orders, width), F32),
            dma((N - 1,)),
            dma((N - 1,)),
            pltpu.VMEM((CHUNKS, orders, everyone, wide), F32),
            dma((CHUNKS, N - 1)),
            dma((CHUNKS, N - 1)),
            dma((CHUNKS,)),
            pltpu.VMEM((orders, everyone, wide), BF16),
            pltpu.VMEM((orders, everyone, wide), BF16),
            pltpu.VMEM((orders, width, wide), F32),
            pltpu.VMEM((orders, 2 * width, wide), BF16),
            pltpu.VMEM((orders, everyone, width), F32),
            pltpu.VMEM((orders, everyone // 2, width), F32),
            dma((2,)),
            pltpu.VMEM((CHIPS - 1, orders, rows, width), F32),
            pltpu.VMEM((CHIPS - 1, orders, rows, width), F32),
            dma((CHIPS - 1,)),
            dma((CHIPS - 1,)),
        ],
        compiler_params=pltpu.CompilerParams(
            collective_id=0, has_side_effects=True, vmem_limit_bytes=60 * 1024 * 1024
        ),
    )(cycles, legendre, weight.reshape(1, rows), jnp.transpose(filters, (1, 2, 0)), hits, flux, order)


def solution(mesh):
    return jax.shard_map(
        body,
        mesh=mesh,
        in_specs=(
            P("order", "blk", None),
            P("order", "blk", None),
            P("blk"),
            P("blk", None, None),
            P("order", None),
            P("order", None, None),
            P("order"),
        ),
        out_specs=P("order", "blk", None),
        check_vma=False,
    )
```

```python
import functools

import jax
import jax.numpy as jnp
from jax import lax
from jax.experimental import pallas as pl
from jax.experimental.pallas import tpu as pltpu
from jax.sharding import PartitionSpec as P

L = 12288
F = 8
S = 8
SIMS = 8
M = 2
Y, X, CORES = 4, 2, 2
CHIPS = Y * X
N = CHIPS * CORES
WIDE = 256
PIECES = ((0, 0, 768), (1, 0, 512), (1, 512, 256))

MESH = pl.DeviceIdType.MESH
F32 = jnp.float32
BF16 = jnp.bfloat16

CHIP_STEPS = ((2, 1), (2, 0), (1, 1), (3, 1), (0, 1), (1, 0), (3, 0))
LINKS = {(0, 0): 0, (0, 1): 1, (1, 0): 1, (3, 0): 1, (2, 0): 2, (1, 1): 2, (3, 1): 2, (2, 1): 3}
STEPS = tuple((dy, dx, dc) for dy, dx in CHIP_STEPS for dc in range(CORES)) + ((0, 0, 1),)


def halves(value):
    high = value.astype(BF16)
    return high, (value - high.astype(F32)).astype(BF16)


def dot(a, b, dims=((1,), (0,))):
    return lax.dot_general(a, b, (dims, ((), ())), preferred_element_type=F32)


def kernel(
    cycles_hbm, legendre_hbm, weight_hbm, filter_hbm, hit_hbm, flux_hbm, order_ref, out_ref,
    own_cycles, own_weight, filters, hits, flux, load_sem,
    injected, injected_t, inj_send, inj_recv, pair_sem, round_sem,
    responses, resp_send, resp_recv,
    blocks, block_send, block_recv, own_sem,
    high, low, harmonics, matched, total, from_core, core_send, core_recv, outgoing, arriving, kept, sum_send, sum_recv,
):
    me = lax.axis_index("blk")
    y, x, core = me // (X * CORES), (me // CORES) % X, me % CORES
    chip = me // CORES
    rows = own_cycles.shape[1]
    half = CHIPS * rows
    degrees = filters.shape[2]

    def chip_at(dy, dx):
        return ((y + dy) % Y) * X + (x + dx) % X

    def at(dy, dx, dc):
        return {"blk": chip_at(dy, dx) * CORES + (core + dc) % CORES}

    barrier = pltpu.get_barrier_semaphore()
    near = [step for step in STEPS if LINKS[step[:2]] <= 1]
    for step in near:
        pl.semaphore_signal(barrier, inc=1, device_id=at(*step), device_id_type=MESH)

    loads = [
        pltpu.make_async_copy(source, target, load_sem.at[i])
        for i, (source, target) in enumerate(
            ((cycles_hbm, own_cycles), (weight_hbm, own_weight), (hit_hbm, hits), (flux_hbm, flux), (filter_hbm, filters))
        )
    ]
    for load in loads:
        load.start()

    own_rows = pl.ds(pl.multiple_of(half + chip * rows, rows), rows)

    def own_copy(q):
        k, first, wide = PIECES[q]
        return pltpu.make_async_copy(
            legendre_hbm.at[k, :, pl.ds(pl.multiple_of(me * degrees + first, 128), wide)],
            blocks.at[k, own_rows, pl.ds(first, wide)],
            own_sem.at[q],
        )

    def block_copy(q, i):
        k, first, wide = PIECES[q]
        dy, dx, dc = STEPS[i]
        there = chip_at(dy, dx) * CORES + (core + dc) % CORES
        return pltpu.make_async_remote_copy(
            src_ref=legendre_hbm.at[k, :, pl.ds(pl.multiple_of(there * degrees + first, 128), wide)],
            dst_ref=blocks.at[
                k, pl.ds(pl.multiple_of((1 - dc) * half + chip * rows, rows), rows), pl.ds(first, wide)
            ],
            send_sem=block_send.at[q, i],
            recv_sem=block_recv.at[q, i],
            device_id={"blk": there},
            device_id_type=MESH,
        )

    for links in range(1, 4):
        if links == 1:
            pl.semaphore_wait(barrier, len(near))
        else:
            pl.semaphore_wait(round_sem.at[links - 2], 3)
        if links < 3:
            for dy, dx in ((0, 1), (1, 0), (3, 0)):
                pl.semaphore_signal(round_sem.at[links - 1], inc=1, device_id=at(dy, dx, 0), device_id_type=MESH)
        for i, step in enumerate(STEPS):
            if LINKS[step[:2]] == links or (links == 1 and step == (0, 0, 1)):
                block_copy(0, i).start()
    own_copy(0).start()

    for load in loads[:4]:
        load.wait()
    row = lax.broadcasted_iota(jnp.int32, (rows, rows), 0)
    lane = lax.broadcasted_iota(jnp.int32, (rows, rows), 1)
    weight = jnp.sum(jnp.where(row == lane, own_weight[...], 0.0), axis=1, keepdims=True)
    for k in range(M):
        clusters = hits.shape[1]
        cycle = me * rows + lax.broadcasted_iota(jnp.int32, (rows, clusters), 0)
        hit = (cycle == hits[k : k + 1, :]).astype(F32)
        added = lax.dot_general(
            hit, flux[k], (((1,), (0,)), ((), ())), precision=lax.Precision.HIGHEST, preferred_element_type=F32
        )
        injected[k, own_rows, :] = weight * (own_cycles[k] + added)

    loads[4].wait()
    degree = me * degrees + lax.broadcasted_iota(jnp.int32, (1, degrees), 1)
    squares = jnp.sum(filters[...] * filters[...], axis=1)
    scale_of = (lax.broadcasted_iota(jnp.int32, (S, 128), 1) // SIMS) % S == lax.broadcasted_iota(jnp.int32, (S, 128), 0)
    for k in range(M):
        factor = jnp.where(degree >= order_ref[k], 2.0 * degree.astype(F32) + 1.0, 0.0)
        response = jnp.sum(squares * factor, axis=1, keepdims=True)
        responses[CHIPS + chip, k : k + 1, :] = jnp.sum(jnp.where(scale_of, response, 0.0), axis=0, keepdims=True)

    inj_copies = [
        pltpu.make_async_remote_copy(
            src_ref=injected.at[:, own_rows, :],
            dst_ref=injected.at[:, own_rows, :],
            send_sem=inj_send.at[i],
            recv_sem=inj_recv.at[i],
            device_id=at(dy, dx, 0),
            device_id_type=MESH,
        )
        for i, (dy, dx) in enumerate(CHIP_STEPS)
    ]
    for copy in inj_copies:
        copy.start()
    resp_copies = [
        pltpu.make_async_remote_copy(
            src_ref=responses.at[CHIPS + chip],
            dst_ref=responses.at[CHIPS + chip],
            send_sem=resp_send.at[i],
            recv_sem=resp_recv.at[i],
            device_id=at(dy, dx, 0),
            device_id_type=MESH,
        )
        for i, (dy, dx) in enumerate(CHIP_STEPS)
    ]
    for copy in resp_copies:
        copy.start()
    for q in range(1, len(PIECES)):
        for i in range(N - 1):
            block_copy(q, i).start()
        own_copy(q).start()

    total[...] = jnp.zeros_like(total)
    for copy in inj_copies:
        copy.wait_recv()
    for copy in resp_copies:
        copy.wait_recv()
    pairs = [
        pltpu.make_async_remote_copy(
            src_ref=source,
            dst_ref=target,
            send_sem=pair_sem.at[i, 0],
            recv_sem=pair_sem.at[i, 1],
            device_id=at(0, 0, 1),
            device_id_type=MESH,
        )
        for i, (source, target) in enumerate(
            (
                (injected.at[:, pl.ds(half, half), :], injected.at[:, pl.ds(0, half), :]),
                (responses.at[pl.ds(CHIPS, CHIPS)], responses.at[pl.ds(0, CHIPS)]),
            )
        )
    ]
    for copy in pairs:
        copy.start()
    for copy in pairs:
        copy.wait_recv()
    for k in range(M):
        turned = jnp.transpose(injected[k])
        turned_high, turned_low = halves(turned)
        injected_t[k, 0:128, :] = turned_high
        injected_t[k, 128:256, :] = turned_low

    def core_copy(k):
        return pltpu.make_async_remote_copy(
            src_ref=total.at[k, pl.ds(0, half), :],
            dst_ref=from_core.at[k],
            send_sem=core_send.at[k],
            recv_sem=core_recv.at[k],
            device_id=at(0, 0, 1),
            device_id_type=MESH,
        )

    def sum_copy(k, i):
        dy, dx = CHIP_STEPS[i]
        return pltpu.make_async_remote_copy(
            src_ref=outgoing.at[k, i],
            dst_ref=arriving.at[k, i],
            send_sem=sum_send.at[k, i],
            recv_sem=sum_recv.at[k, i],
            device_id=at(dy, dx, 0),
            device_id_type=MESH,
        )

    def send_sums(k):
        core_copy(k).wait_recv()
        for i, (dy, dx) in enumerate(CHIP_STEPS):
            there = chip_at(dy, dx) * rows
            outgoing[k, i] = (
                total[k, pl.ds(pl.multiple_of(half + there, rows), rows), :]
                + from_core[k, pl.ds(pl.multiple_of(there, rows), rows), :]
            )
        kept[k] = total[k, own_rows, :] + from_core[k, pl.ds(pl.multiple_of(chip * rows, rows), rows), :]
        for i in range(CHIPS - 1):
            sum_copy(k, i).start()

    def take_sums(k):
        value = kept[k]
        for i in range(CHIPS - 1):
            sum_copy(k, i).wait_recv()
            value = value + arriving[k, i]
        out_ref[k] = value * scale[k : k + 1, :]

    parts = degrees // WIDE

    def part_of(n, carry):
        k = n // parts
        for q, (slot, first, _) in enumerate(PIECES):

            @pl.when(n == slot * parts + first // WIDE)
            def _():
                own_copy(q).wait()
                for i in range(N - 1):
                    block_copy(q, i).wait_recv()

        start = pl.multiple_of((n % parts) * WIDE, WIDE)
        degree = me * degrees + start + lax.broadcasted_iota(jnp.int32, (1, WIDE), 1)
        block_high, block_low = halves(blocks[k, :, pl.ds(start, WIDE)])
        high[...] = block_high
        low[...] = block_low
        first = dot(injected_t[k], high[...])
        second = dot(injected_t[k, 0:128], low[...])
        value = first[0:128] + first[128:256] + second
        harmonics[...] = jnp.where(degree >= order_ref[k], value, 0.0)
        for t in range(WIDE // 128):
            lanes = pl.ds(t * 128, 128)
            for s in range(S):
                sums = [None, None]
                for f in range(F):
                    row = filters[s, f : f + 1, pl.ds(start + t * 128, 128)]
                    for p in range(2):
                        term = row * harmonics[pl.ds((p * F + f) * SIMS, SIMS), lanes]
                        sums[p] = term if f == 0 else sums[p] + term
                for p in range(2):
                    out_high, out_low = halves(sums[p])
                    matched[pl.ds((p * S + s) * SIMS, SIMS), lanes] = out_high
                    matched[pl.ds(128 + (p * S + s) * SIMS, SIMS), lanes] = out_low
        for part in range(2):
            span = pl.ds(part * half, half)
            both = dot(high[span, :], matched[...], ((1,), (1,)))
            third = dot(low[span, :], matched[0:128], ((1,), (1,)))
            total[k, span, :] += both[:, 0:128] + both[:, 128:256] + third
            if part == 0:

                @pl.when(n % parts == parts - 1)
                def _():
                    core_copy(k).start()

        @pl.when(n == parts)
        def _():
            send_sums(0)

        return carry

    lax.fori_loop(0, M * parts, part_of, 0)

    send_sums(1)
    scale = L / jnp.sqrt(jnp.sum(responses[...], axis=0))
    take_sums(0)
    take_sums(1)

    for copy in inj_copies + resp_copies + pairs:
        copy.wait_send()
    for k in range(M):
        core_copy(k).wait_send()
        for i in range(CHIPS - 1):
            sum_copy(k, i).wait_send()
    for q in range(len(PIECES)):
        for i in range(N - 1):
            block_copy(q, i).wait_send()


def body(cycles, legendre, weight, filters, hits, flux, order):
    orders, rows, width = cycles.shape
    degrees = filters.shape[0]
    clusters = hits.shape[1]
    everyone = N * rows
    dma = pltpu.SemaphoreType.DMA
    anywhere = pl.BlockSpec(memory_space=pl.ANY)
    return pl.pallas_call(
        kernel,
        out_shape=jax.ShapeDtypeStruct(cycles.shape, F32),
        in_specs=[anywhere] * 6 + [pl.BlockSpec(memory_space=pltpu.SMEM)],
        out_specs=pl.BlockSpec(memory_space=pltpu.VMEM),
        scratch_shapes=[
            pltpu.VMEM((orders, rows, width), F32),
            pltpu.VMEM((1, rows), F32),
            pltpu.VMEM((S, F, degrees), F32),
            pltpu.VMEM((orders, clusters), jnp.int32),
            pltpu.VMEM((orders, clusters, width), F32),
            dma((5,)),
            pltpu.VMEM((orders, everyone, width), F32),
            pltpu.VMEM((orders, 2 * width, everyone), BF16),
            dma((CHIPS - 1,)),
            dma((CHIPS - 1,)),
            dma((2, 2)),
            pltpu.SemaphoreType.REGULAR((2,)),
            pltpu.VMEM((N, orders, width), F32),
            dma((CHIPS - 1,)),
            dma((CHIPS - 1,)),
            pltpu.VMEM((orders, everyone, degrees), F32),
            dma((len(PIECES), N - 1)),
            dma((len(PIECES), N - 1)),
            dma((len(PIECES),)),
            pltpu.VMEM((everyone, WIDE), BF16),
            pltpu.VMEM((everyone, WIDE), BF16),
            pltpu.VMEM((width, WIDE), F32),
            pltpu.VMEM((2 * width, WIDE), BF16),
            pltpu.VMEM((orders, everyone, width), F32),
            pltpu.VMEM((orders, everyone // 2, width), F32),
            dma((orders,)),
            dma((orders,)),
            pltpu.VMEM((orders, CHIPS - 1, rows, width), F32),
            pltpu.VMEM((orders, CHIPS - 1, rows, width), F32),
            pltpu.VMEM((orders, rows, width), F32),
            dma((orders, CHIPS - 1)),
            dma((orders, CHIPS - 1)),
        ],
        compiler_params=pltpu.CompilerParams(
            collective_id=0, has_side_effects=True, vmem_limit_bytes=60 * 1024 * 1024
        ),
    )(cycles, legendre, weight.reshape(1, rows), jnp.transpose(filters, (1, 2, 0)), hits, flux, order)


def solution(mesh):
    return jax.shard_map(
        body,
        mesh=mesh,
        in_specs=(
            P("order", "blk", None),
            P("order", "blk", None),
            P("blk"),
            P("blk", None, None),
            P("order", None),
            P("order", None, None),
            P("order"),
        ),
        out_specs=P("order", "blk", None),
        check_vma=False,
    )
```

```python
import functools

import jax
import jax.numpy as jnp
from jax import lax
from jax.experimental import pallas as pl
from jax.experimental.pallas import tpu as pltpu
from jax.sharding import PartitionSpec as P

L = 12288
F = 8
S = 8
SIMS = 8
M = 2
Y, X, CORES = 4, 2, 2
CHIPS = Y * X
N = CHIPS * CORES
WIDE = 256
PIECES = ((0, 0, 768), (1, 0, 512), (1, 512, 256))

MESH = pl.DeviceIdType.MESH
F32 = jnp.float32
BF16 = jnp.bfloat16

CHIP_STEPS = ((2, 1), (2, 0), (1, 1), (3, 1), (0, 1), (1, 0), (3, 0))
STEPS = tuple((dy, dx, dc) for dy, dx in CHIP_STEPS for dc in range(CORES)) + ((0, 0, 1),)


def halves(value):
    high = value.astype(BF16)
    return high, (value - high.astype(F32)).astype(BF16)


def dot(a, b, dims=((1,), (0,))):
    return lax.dot_general(a, b, (dims, ((), ())), preferred_element_type=F32)


def kernel(
    cycles_hbm, legendre_hbm, weight_hbm, filter_hbm, hit_hbm, flux_hbm, order_hbm, out_ref,
    order_ref, own_cycles, own_weight, filters, hits, flux, load_sem,
    injected, injected_t, inj_send, inj_recv, pair_sem,
    responses, resp_send, resp_recv,
    blocks, block_send, block_recv, own_sem,
    high, low, harmonics, matched, total, from_core, core_send, core_recv, outgoing, arriving, kept, sum_send, sum_recv,
):
    me = lax.axis_index("blk")
    y, x, core = me // (X * CORES), (me // CORES) % X, me % CORES
    chip = me // CORES
    rows = own_cycles.shape[1]
    half = CHIPS * rows
    degrees = filters.shape[2]

    def chip_at(dy, dx):
        return ((y + dy) % Y) * X + (x + dx) % X

    def at(dy, dx, dc):
        return {"blk": chip_at(dy, dx) * CORES + (core + dc) % CORES}

    barrier = pltpu.get_barrier_semaphore()
    for step in STEPS:
        pl.semaphore_signal(barrier, inc=1, device_id=at(*step), device_id_type=MESH)

    loads = [
        pltpu.make_async_copy(source, target, load_sem.at[i])
        for i, (source, target) in enumerate(
            ((cycles_hbm, own_cycles), (weight_hbm, own_weight), (hit_hbm, hits), (flux_hbm, flux), (filter_hbm, filters), (order_hbm, order_ref))
        )
    ]
    for load in loads:
        load.start()

    own_rows = pl.ds(pl.multiple_of(half + chip * rows, rows), rows)

    def own_copy(q):
        k, first, wide = PIECES[q]
        return pltpu.make_async_copy(
            legendre_hbm.at[k, :, pl.ds(pl.multiple_of(me * degrees + first, 128), wide)],
            blocks.at[k, own_rows, pl.ds(first, wide)],
            own_sem.at[q],
        )

    def block_copy(q, i):
        k, first, wide = PIECES[q]
        dy, dx, dc = STEPS[i]
        there = chip_at(dy, dx) * CORES + (core + dc) % CORES
        return pltpu.make_async_remote_copy(
            src_ref=legendre_hbm.at[k, :, pl.ds(pl.multiple_of(there * degrees + first, 128), wide)],
            dst_ref=blocks.at[
                k, pl.ds(pl.multiple_of((1 - dc) * half + chip * rows, rows), rows), pl.ds(first, wide)
            ],
            send_sem=block_send.at[q, i],
            recv_sem=block_recv.at[q, i],
            device_id={"blk": there},
            device_id_type=MESH,
        )

    pl.semaphore_wait(barrier, N - 1)
    for i in range(N - 1):
        block_copy(0, i).start()
    own_copy(0).start()

    for load in loads[:4]:
        load.wait()
    row = lax.broadcasted_iota(jnp.int32, (rows, rows), 0)
    lane = lax.broadcasted_iota(jnp.int32, (rows, rows), 1)
    weight = jnp.sum(jnp.where(row == lane, own_weight[...], 0.0), axis=1, keepdims=True)
    for k in range(M):
        clusters = hits.shape[1]
        cycle = me * rows + lax.broadcasted_iota(jnp.int32, (rows, clusters), 0)
        hit = (cycle == hits[k : k + 1, :]).astype(F32)
        added = lax.dot_general(
            hit, flux[k], (((1,), (0,)), ((), ())), precision=lax.Precision.HIGHEST, preferred_element_type=F32
        )
        injected[k, own_rows, :] = weight * (own_cycles[k] + added)

    loads[4].wait()
    loads[5].wait()
    degree = me * degrees + lax.broadcasted_iota(jnp.int32, (1, degrees), 1)
    squares = jnp.sum(filters[...] * filters[...], axis=1)
    scale_of = (lax.broadcasted_iota(jnp.int32, (S, 128), 1) // SIMS) % S == lax.broadcasted_iota(jnp.int32, (S, 128), 0)
    for k in range(M):
        factor = jnp.where(degree >= order_ref[k], 2.0 * degree.astype(F32) + 1.0, 0.0)
        response = jnp.sum(squares * factor, axis=1, keepdims=True)
        responses[CHIPS + chip, k : k + 1, :] = jnp.sum(jnp.where(scale_of, response, 0.0), axis=0, keepdims=True)

    inj_copies = [
        pltpu.make_async_remote_copy(
            src_ref=injected.at[:, own_rows, :],
            dst_ref=injected.at[:, own_rows, :],
            send_sem=inj_send.at[i],
            recv_sem=inj_recv.at[i],
            device_id=at(dy, dx, 0),
            device_id_type=MESH,
        )
        for i, (dy, dx) in enumerate(CHIP_STEPS)
    ]
    for copy in inj_copies:
        copy.start()
    resp_copies = [
        pltpu.make_async_remote_copy(
            src_ref=responses.at[CHIPS + chip],
            dst_ref=responses.at[CHIPS + chip],
            send_sem=resp_send.at[i],
            recv_sem=resp_recv.at[i],
            device_id=at(dy, dx, 0),
            device_id_type=MESH,
        )
        for i, (dy, dx) in enumerate(CHIP_STEPS)
    ]
    for copy in resp_copies:
        copy.start()
    for q in range(1, len(PIECES)):
        for i in range(N - 1):
            block_copy(q, i).start()
        own_copy(q).start()

    total[...] = jnp.zeros_like(total)
    for copy in inj_copies:
        copy.wait_recv()
    for copy in resp_copies:
        copy.wait_recv()
    pairs = [
        pltpu.make_async_remote_copy(
            src_ref=source,
            dst_ref=target,
            send_sem=pair_sem.at[i, 0],
            recv_sem=pair_sem.at[i, 1],
            device_id=at(0, 0, 1),
            device_id_type=MESH,
        )
        for i, (source, target) in enumerate(
            (
                (injected.at[:, pl.ds(half, half), :], injected.at[:, pl.ds(0, half), :]),
                (responses.at[pl.ds(CHIPS, CHIPS)], responses.at[pl.ds(0, CHIPS)]),
            )
        )
    ]
    for copy in pairs:
        copy.start()
    for copy in pairs:
        copy.wait_recv()
    for k in range(M):
        turned = jnp.transpose(injected[k])
        turned_high, turned_low = halves(turned)
        injected_t[k, 0:128, :] = turned_high
        injected_t[k, 128:256, :] = turned_low

    def core_copy(k):
        return pltpu.make_async_remote_copy(
            src_ref=total.at[k, pl.ds(0, half), :],
            dst_ref=from_core.at[k],
            send_sem=core_send.at[k],
            recv_sem=core_recv.at[k],
            device_id=at(0, 0, 1),
            device_id_type=MESH,
        )

    def sum_copy(k, i):
        dy, dx = CHIP_STEPS[i]
        return pltpu.make_async_remote_copy(
            src_ref=outgoing.at[k, i],
            dst_ref=arriving.at[k, i],
            send_sem=sum_send.at[k, i],
            recv_sem=sum_recv.at[k, i],
            device_id=at(dy, dx, 0),
            device_id_type=MESH,
        )

    def send_sums(k):
        core_copy(k).wait_recv()
        for i, (dy, dx) in enumerate(CHIP_STEPS):
            there = chip_at(dy, dx) * rows
            outgoing[k, i] = (
                total[k, pl.ds(pl.multiple_of(half + there, rows), rows), :]
                + from_core[k, pl.ds(pl.multiple_of(there, rows), rows), :]
            )
        kept[k] = total[k, own_rows, :] + from_core[k, pl.ds(pl.multiple_of(chip * rows, rows), rows), :]
        for i in range(CHIPS - 1):
            sum_copy(k, i).start()

    def take_sums(k):
        value = kept[k]
        for i in range(CHIPS - 1):
            sum_copy(k, i).wait_recv()
            value = value + arriving[k, i]
        out_ref[k] = value * scale[k : k + 1, :]

    parts = degrees // WIDE

    def part_of(n, carry):
        k = n // parts
        for q, (slot, first, _) in enumerate(PIECES):

            @pl.when(n == slot * parts + first // WIDE)
            def _():
                own_copy(q).wait()
                for i in range(N - 1):
                    block_copy(q, i).wait_recv()

        start = pl.multiple_of((n % parts) * WIDE, WIDE)
        degree = me * degrees + start + lax.broadcasted_iota(jnp.int32, (1, WIDE), 1)
        block_high, block_low = halves(blocks[k, :, pl.ds(start, WIDE)])
        high[...] = block_high
        low[...] = block_low
        first = dot(injected_t[k], high[...])
        second = dot(injected_t[k, 0:128], low[...])
        value = first[0:128] + first[128:256] + second
        harmonics[...] = jnp.where(degree >= order_ref[k], value, 0.0)
        for t in range(WIDE // 128):
            lanes = pl.ds(t * 128, 128)
            for s in range(S):
                sums = [None, None]
                for f in range(F):
                    row = filters[s, f : f + 1, pl.ds(start + t * 128, 128)]
                    for p in range(2):
                        term = row * harmonics[pl.ds((p * F + f) * SIMS, SIMS), lanes]
                        sums[p] = term if f == 0 else sums[p] + term
                for p in range(2):
                    out_high, out_low = halves(sums[p])
                    matched[pl.ds((p * S + s) * SIMS, SIMS), lanes] = out_high
                    matched[pl.ds(128 + (p * S + s) * SIMS, SIMS), lanes] = out_low
        for part in range(2):
            span = pl.ds(part * half, half)
            both = dot(high[span, :], matched[...], ((1,), (1,)))
            third = dot(low[span, :], matched[0:128], ((1,), (1,)))
            total[k, span, :] += both[:, 0:128] + both[:, 128:256] + third
            if part == 0:

                @pl.when(n % parts == parts - 1)
                def _():
                    core_copy(k).start()

        @pl.when(n == parts)
        def _():
            send_sums(0)

        return carry

    lax.fori_loop(0, M * parts, part_of, 0)

    send_sums(1)
    scale = L / jnp.sqrt(jnp.sum(responses[...], axis=0))
    take_sums(0)
    take_sums(1)

    for copy in inj_copies + resp_copies + pairs:
        copy.wait_send()
    for k in range(M):
        core_copy(k).wait_send()
        for i in range(CHIPS - 1):
            sum_copy(k, i).wait_send()
    for q in range(len(PIECES)):
        for i in range(N - 1):
            block_copy(q, i).wait_send()


def body(cycles, legendre, weight, filters, hits, flux, order):
    orders, rows, width = cycles.shape
    degrees = filters.shape[0]
    clusters = hits.shape[1]
    everyone = N * rows
    dma = pltpu.SemaphoreType.DMA
    anywhere = pl.BlockSpec(memory_space=pl.ANY)
    return pl.pallas_call(
        kernel,
        out_shape=pltpu.VMEM(cycles.shape, F32),
        in_specs=[anywhere] * 7,
        out_specs=pl.BlockSpec(memory_space=pltpu.VMEM),
        scratch_shapes=[
            pltpu.SMEM((orders,), jnp.int32),
            pltpu.VMEM((orders, rows, width), F32),
            pltpu.VMEM((1, rows), F32),
            pltpu.VMEM((S, F, degrees), F32),
            pltpu.VMEM((orders, clusters), jnp.int32),
            pltpu.VMEM((orders, clusters, width), F32),
            dma((6,)),
            pltpu.VMEM((orders, everyone, width), F32),
            pltpu.VMEM((orders, 2 * width, everyone), BF16),
            dma((CHIPS - 1,)),
            dma((CHIPS - 1,)),
            dma((2, 2)),
            pltpu.VMEM((N, orders, width), F32),
            dma((CHIPS - 1,)),
            dma((CHIPS - 1,)),
            pltpu.VMEM((orders, everyone, degrees), F32),
            dma((len(PIECES), N - 1)),
            dma((len(PIECES), N - 1)),
            dma((len(PIECES),)),
            pltpu.VMEM((everyone, WIDE), BF16),
            pltpu.VMEM((everyone, WIDE), BF16),
            pltpu.VMEM((width, WIDE), F32),
            pltpu.VMEM((2 * width, WIDE), BF16),
            pltpu.VMEM((orders, everyone, width), F32),
            pltpu.VMEM((orders, everyone // 2, width), F32),
            dma((orders,)),
            dma((orders,)),
            pltpu.VMEM((orders, CHIPS - 1, rows, width), F32),
            pltpu.VMEM((orders, CHIPS - 1, rows, width), F32),
            pltpu.VMEM((orders, rows, width), F32),
            dma((orders, CHIPS - 1)),
            dma((orders, CHIPS - 1)),
        ],
        compiler_params=pltpu.CompilerParams(
            collective_id=0, has_side_effects=True, vmem_limit_bytes=60 * 1024 * 1024
        ),
    )(cycles, legendre, weight.reshape(1, rows), jnp.transpose(filters, (1, 2, 0)), hits, flux, order)


def solution(mesh):
    return jax.shard_map(
        body,
        mesh=mesh,
        in_specs=(
            P("order", "blk", None),
            P("order", "blk", None),
            P("blk"),
            P("blk", None, None),
            P("order", None),
            P("order", None, None),
            P("order"),
        ),
        out_specs=P("order", "blk", None),
        check_vma=False,
    )
```

```python
import functools

import jax
import jax.numpy as jnp
from jax import lax
from jax.experimental import pallas as pl
from jax.experimental.pallas import tpu as pltpu
from jax.sharding import PartitionSpec as P

L = 12288
F = 8
S = 8
SIMS = 8
M = 2
Y, X, CORES = 4, 2, 2
CHIPS = Y * X
N = CHIPS * CORES
WIDE = 256
PIECES = ((0, 0, 768), (1, 0, 512), (1, 512, 256))

MESH = pl.DeviceIdType.MESH
F32 = jnp.float32
BF16 = jnp.bfloat16

CHIP_STEPS = ((2, 1), (2, 0), (1, 1), (3, 1), (0, 1), (1, 0), (3, 0))
RELAYS = ((0, 1), (2, 0), (1, 0), (3, 0))
STEPS = tuple((dy, dx, dc) for dy, dx in CHIP_STEPS for dc in range(CORES)) + ((0, 0, 1),)


def halves(value):
    high = value.astype(BF16)
    return high, (value - high.astype(F32)).astype(BF16)


def take(ref, sem):
    pltpu.make_async_copy(ref, ref, sem).wait()


def dot(a, b, dims=((1,), (0,))):
    return lax.dot_general(a, b, (dims, ((), ())), preferred_element_type=F32)


def kernel(
    cycles_hbm, legendre_hbm, weight_hbm, filter_hbm, hit_hbm, flux_hbm, order_hbm, out_ref,
    order_ref, own_cycles, own_weight, filters, hits, flux, load_sem,
    injected, injected_t, inj_send, inj_recv, pair_sem,
    responses, resp_send, resp_recv,
    blocks, block_send, block_recv,
    high, low, harmonics, matched, total, from_core, core_send, core_recv, outgoing, arriving, kept, sum_send, sum_recv,
):
    me = lax.axis_index("blk")
    y, x, core = me // (X * CORES), (me // CORES) % X, me % CORES
    chip = me // CORES
    rows = own_cycles.shape[1]
    half = CHIPS * rows
    degrees = filters.shape[2]

    def chip_at(dy, dx):
        return ((y + dy) % Y) * X + (x + dx) % X

    def at(dy, dx, dc):
        return {"blk": chip_at(dy, dx) * CORES + (core + dc) % CORES}

    barrier = pltpu.get_barrier_semaphore()
    for step in STEPS:
        pl.semaphore_signal(barrier, inc=1, device_id=at(*step), device_id_type=MESH)

    loads = [
        pltpu.make_async_copy(source, target, load_sem.at[i])
        for i, (source, target) in enumerate(
            ((cycles_hbm, own_cycles), (weight_hbm, own_weight), (hit_hbm, hits), (flux_hbm, flux), (filter_hbm, filters), (order_hbm, order_ref))
        )
    ]
    for load in loads:
        load.start()

    own_rows = pl.ds(pl.multiple_of(half + chip * rows, rows), rows)

    def own_copy(q):
        k, first, wide = PIECES[q]
        return pltpu.make_async_copy(
            legendre_hbm.at[k, :, pl.ds(pl.multiple_of(me * degrees + first, 128), wide)],
            blocks.at[k, own_rows, pl.ds(first, wide)],
            block_recv.at[q],
        )

    def block_copy(q, i):
        k, first, wide = PIECES[q]
        dy, dx, dc = STEPS[i]
        there = chip_at(dy, dx) * CORES + (core + dc) % CORES
        return pltpu.make_async_remote_copy(
            src_ref=legendre_hbm.at[k, :, pl.ds(pl.multiple_of(there * degrees + first, 128), wide)],
            dst_ref=blocks.at[
                k, pl.ds(pl.multiple_of((1 - dc) * half + chip * rows, rows), rows), pl.ds(first, wide)
            ],
            send_sem=block_send.at[0],
            recv_sem=block_recv.at[q],
            device_id={"blk": there},
            device_id_type=MESH,
        )

    for load in loads[:4]:
        load.wait()
    row = lax.broadcasted_iota(jnp.int32, (rows, rows), 0)
    lane = lax.broadcasted_iota(jnp.int32, (rows, rows), 1)
    weight = jnp.sum(jnp.where(row == lane, own_weight[...], 0.0), axis=1, keepdims=True)
    for k in range(M):
        clusters = hits.shape[1]
        cycle = me * rows + lax.broadcasted_iota(jnp.int32, (rows, clusters), 0)
        hit = (cycle == hits[k : k + 1, :]).astype(F32)
        added = lax.dot_general(
            hit, flux[k], (((1,), (0,)), ((), ())), precision=lax.Precision.HIGHEST, preferred_element_type=F32
        )
        injected[k, own_rows, :] = weight * (own_cycles[k] + added)

    across = chip_at(0, 1)

    def inj_copy(i):
        source, (dy, dx) = ((chip, RELAYS[i]) if i < 4 else (across, RELAYS[i - 3]))
        place = injected.at[:, pl.ds(pl.multiple_of(half + source * rows, rows), rows), :]
        return pltpu.make_async_remote_copy(
            src_ref=place,
            dst_ref=place,
            send_sem=inj_send.at[0],
            recv_sem=inj_recv.at[0 if i == 0 else 1],
            device_id=at(dy, dx, 0),
            device_id_type=MESH,
        )

    pl.semaphore_wait(barrier, N - 1)
    for i in range(4):
        inj_copy(i).start()
    for i in range(N - 1):
        block_copy(0, i).start()
    own_copy(0).start()

    loads[4].wait()
    loads[5].wait()
    degree = me * degrees + lax.broadcasted_iota(jnp.int32, (1, degrees), 1)
    squares = jnp.sum(filters[...] * filters[...], axis=1)
    scale_of = (lax.broadcasted_iota(jnp.int32, (S, 128), 1) // SIMS) % S == lax.broadcasted_iota(jnp.int32, (S, 128), 0)
    for k in range(M):
        factor = jnp.where(degree >= order_ref[k], 2.0 * degree.astype(F32) + 1.0, 0.0)
        response = jnp.sum(squares * factor, axis=1, keepdims=True)
        responses[CHIPS + chip, k : k + 1, :] = jnp.sum(jnp.where(scale_of, response, 0.0), axis=0, keepdims=True)

    resp_copies = [
        pltpu.make_async_remote_copy(
            src_ref=responses.at[CHIPS + chip],
            dst_ref=responses.at[CHIPS + chip],
            send_sem=resp_send.at[0],
            recv_sem=resp_recv.at[0],
            device_id=at(dy, dx, 0),
            device_id_type=MESH,
        )
        for dy, dx in CHIP_STEPS
    ]
    for copy in resp_copies:
        copy.start()
    inj_copy(0).wait_recv()
    for i in range(4, CHIPS - 1):
        inj_copy(i).start()
    for q in range(1, len(PIECES)):
        for i in range(N - 1):
            block_copy(q, i).start()
        own_copy(q).start()

    total[...] = jnp.zeros_like(total)
    take(injected.at[:, pl.ds(0, (CHIPS - 2) * rows), :], inj_recv.at[1])
    take(responses.at[pl.ds(0, CHIPS - 1)], resp_recv.at[0])
    pairs = [
        pltpu.make_async_remote_copy(
            src_ref=source,
            dst_ref=target,
            send_sem=pair_sem.at[i, 0],
            recv_sem=pair_sem.at[i, 1],
            device_id=at(0, 0, 1),
            device_id_type=MESH,
        )
        for i, (source, target) in enumerate(
            (
                (injected.at[:, pl.ds(half, half), :], injected.at[:, pl.ds(0, half), :]),
                (responses.at[pl.ds(CHIPS, CHIPS)], responses.at[pl.ds(0, CHIPS)]),
            )
        )
    ]
    for copy in pairs:
        copy.start()
    for copy in pairs:
        copy.wait_recv()
    for k in range(M):
        turned = jnp.transpose(injected[k])
        turned_high, turned_low = halves(turned)
        injected_t[k, 0:128, :] = turned_high
        injected_t[k, 128:256, :] = turned_low

    def core_copy(k):
        return pltpu.make_async_remote_copy(
            src_ref=total.at[k, pl.ds(0, half), :],
            dst_ref=from_core.at[k],
            send_sem=core_send.at[k],
            recv_sem=core_recv.at[k],
            device_id=at(0, 0, 1),
            device_id_type=MESH,
        )

    def sum_copy(k, i):
        dy, dx = CHIP_STEPS[i]
        return pltpu.make_async_remote_copy(
            src_ref=outgoing.at[k, i],
            dst_ref=arriving.at[k, i],
            send_sem=sum_send.at[k],
            recv_sem=sum_recv.at[k],
            device_id=at(dy, dx, 0),
            device_id_type=MESH,
        )

    def send_sums(k):
        core_copy(k).wait_recv()
        for i, (dy, dx) in enumerate(CHIP_STEPS):
            there = chip_at(dy, dx) * rows
            outgoing[k, i] = (
                total[k, pl.ds(pl.multiple_of(half + there, rows), rows), :]
                + from_core[k, pl.ds(pl.multiple_of(there, rows), rows), :]
            )
        kept[k] = total[k, own_rows, :] + from_core[k, pl.ds(pl.multiple_of(chip * rows, rows), rows), :]
        for i in range(CHIPS - 1):
            sum_copy(k, i).start()

    def take_sums(k):
        value = kept[k]
        take(arriving.at[k], sum_recv.at[k])
        for i in range(CHIPS - 1):
            value = value + arriving[k, i]
        out_ref[k] = value * scale[k : k + 1, :]

    parts = degrees // WIDE

    def part_of(n, carry):
        k = n // parts
        for q, (slot, first, wide) in enumerate(PIECES):

            @pl.when(n == slot * parts + first // WIDE)
            def _():
                take(blocks.at[slot, :, pl.ds(first, wide)], block_recv.at[q])

        start = pl.multiple_of((n % parts) * WIDE, WIDE)
        degree = me * degrees + start + lax.broadcasted_iota(jnp.int32, (1, WIDE), 1)
        block_high, block_low = halves(blocks[k, :, pl.ds(start, WIDE)])
        high[...] = block_high
        low[...] = block_low
        first = dot(injected_t[k], high[...])
        second = dot(injected_t[k, 0:128], low[...])
        value = first[0:128] + first[128:256] + second
        harmonics[...] = jnp.where(degree >= order_ref[k], value, 0.0)
        for t in range(WIDE // 128):
            lanes = pl.ds(t * 128, 128)
            for s in range(S):
                sums = [None, None]
                for f in range(F):
                    row = filters[s, f : f + 1, pl.ds(start + t * 128, 128)]
                    for p in range(2):
                        term = row * harmonics[pl.ds((p * F + f) * SIMS, SIMS), lanes]
                        sums[p] = term if f == 0 else sums[p] + term
                for p in range(2):
                    out_high, out_low = halves(sums[p])
                    matched[pl.ds((p * S + s) * SIMS, SIMS), lanes] = out_high
                    matched[pl.ds(128 + (p * S + s) * SIMS, SIMS), lanes] = out_low
        for part in range(2):
            span = pl.ds(part * half, half)
            both = dot(high[span, :], matched[...], ((1,), (1,)))
            third = dot(low[span, :], matched[0:128], ((1,), (1,)))
            total[k, span, :] += both[:, 0:128] + both[:, 128:256] + third
            if part == 0:

                @pl.when(n % parts == parts - 1)
                def _():
                    core_copy(k).start()

        @pl.when(n == parts)
        def _():
            send_sums(0)

        return carry

    lax.fori_loop(0, M * parts, part_of, 0)

    send_sums(1)
    scale = L / jnp.sqrt(jnp.sum(responses[...], axis=0))
    take_sums(0)
    take_sums(1)

    take(injected.at[:, pl.ds(0, (CHIPS - 1) * rows), :], inj_send.at[0])
    take(responses.at[pl.ds(0, CHIPS - 1)], resp_send.at[0])
    for copy in pairs:
        copy.wait_send()
    for k in range(M):
        core_copy(k).wait_send()
        take(outgoing.at[k], sum_send.at[k])
    take(blocks.at[:, pl.ds(0, (N - 1) * rows), :], block_send.at[0])


def body(cycles, legendre, weight, filters, hits, flux, order):
    orders, rows, width = cycles.shape
    degrees = filters.shape[0]
    clusters = hits.shape[1]
    everyone = N * rows
    dma = pltpu.SemaphoreType.DMA
    anywhere = pl.BlockSpec(memory_space=pl.ANY)
    return pl.pallas_call(
        kernel,
        out_shape=pltpu.VMEM(cycles.shape, F32),
        in_specs=[anywhere] * 7,
        out_specs=pl.BlockSpec(memory_space=pltpu.VMEM),
        scratch_shapes=[
            pltpu.SMEM((orders,), jnp.int32),
            pltpu.VMEM((orders, rows, width), F32),
            pltpu.VMEM((1, rows), F32),
            pltpu.VMEM((S, F, degrees), F32),
            pltpu.VMEM((orders, clusters), jnp.int32),
            pltpu.VMEM((orders, clusters, width), F32),
            dma((6,)),
            pltpu.VMEM((orders, everyone, width), F32),
            pltpu.VMEM((orders, 2 * width, everyone), BF16),
            dma((1,)),
            dma((2,)),
            dma((2, 2)),
            pltpu.VMEM((N, orders, width), F32),
            dma((1,)),
            dma((1,)),
            pltpu.VMEM((orders, everyone, degrees), F32),
            dma((1,)),
            dma((len(PIECES),)),
            pltpu.VMEM((everyone, WIDE), BF16),
            pltpu.VMEM((everyone, WIDE), BF16),
            pltpu.VMEM((width, WIDE), F32),
            pltpu.VMEM((2 * width, WIDE), BF16),
            pltpu.VMEM((orders, everyone, width), F32),
            pltpu.VMEM((orders, everyone // 2, width), F32),
            dma((orders,)),
            dma((orders,)),
            pltpu.VMEM((orders, CHIPS - 1, rows, width), F32),
            pltpu.VMEM((orders, CHIPS - 1, rows, width), F32),
            pltpu.VMEM((orders, rows, width), F32),
            dma((orders,)),
            dma((orders,)),
        ],
        compiler_params=pltpu.CompilerParams(
            collective_id=0, has_side_effects=True, vmem_limit_bytes=60 * 1024 * 1024
        ),
    )(cycles, legendre, weight.reshape(1, rows), jnp.transpose(filters, (1, 2, 0)), hits, flux, order)


def solution(mesh):
    return jax.shard_map(
        body,
        mesh=mesh,
        in_specs=(
            P("order", "blk", None),
            P("order", "blk", None),
            P("blk"),
            P("blk", None, None),
            P("order", None),
            P("order", None, None),
            P("order"),
        ),
        out_specs=P("order", "blk", None),
        check_vma=False,
    )
```

```python
import functools

import jax
import jax.numpy as jnp
from jax import lax
from jax.experimental import pallas as pl
from jax.experimental.pallas import tpu as pltpu
from jax.sharding import PartitionSpec as P

L = 12288
F = 8
S = 8
SIMS = 8
M = 2
Y, X, CORES = 4, 2, 2
CHIPS = Y * X
N = CHIPS * CORES
WIDE = 256
PIECES = ((0, 0, 768), (1, 0, 512), (1, 512, 256))

MESH = pl.DeviceIdType.MESH
F32 = jnp.float32
BF16 = jnp.bfloat16

CHIP_STEPS = ((2, 1), (2, 0), (1, 1), (3, 1), (0, 1), (1, 0), (3, 0))
RELAYS = ((0, 1), (2, 0), (1, 0), (3, 0))
STEPS = tuple((dy, dx, dc) for dy, dx in CHIP_STEPS for dc in range(CORES)) + ((0, 0, 1),)


def halves(value):
    high = value.astype(BF16)
    return high, (value - high.astype(F32)).astype(BF16)


def take(ref, sem):
    pltpu.make_async_copy(ref, ref, sem).wait()


def dot(a, b, dims=((1,), (0,))):
    return lax.dot_general(a, b, (dims, ((), ())), preferred_element_type=F32)


def kernel(
    cycles_hbm, legendre_hbm, weight_hbm, filter_hbm, hit_hbm, flux_hbm, order_hbm, out_ref,
    order_ref, own_cycles, own_weight, filters, hits, flux, load_sem,
    injected, injected_t, inj_send, inj_recv, pair_sem,
    responses, resp_send, resp_recv,
    blocks, block_send, block_recv,
    high, low, harmonics, matched, total, from_core, core_send, core_recv, outgoing, arriving, kept, sum_send, sum_recv,
):
    me = lax.axis_index("blk")
    y, x, core = me // (X * CORES), (me // CORES) % X, me % CORES
    chip = me // CORES
    rows = own_cycles.shape[1]
    half = CHIPS * rows
    degrees = filters.shape[2]

    def chip_at(dy, dx):
        return ((y + dy) % Y) * X + (x + dx) % X

    def at(dy, dx, dc):
        return {"blk": chip_at(dy, dx) * CORES + (core + dc) % CORES}

    barrier = pltpu.get_barrier_semaphore()
    for step in STEPS:
        pl.semaphore_signal(barrier, inc=1, device_id=at(*step), device_id_type=MESH)

    loads = [
        pltpu.make_async_copy(source, target, load_sem.at[i])
        for i, (source, target) in enumerate(
            ((cycles_hbm, own_cycles), (weight_hbm, own_weight), (hit_hbm, hits), (flux_hbm, flux), (filter_hbm, filters), (order_hbm, order_ref))
        )
    ]
    for load in loads:
        load.start()

    own_rows = pl.ds(pl.multiple_of(half + chip * rows, rows), rows)

    def own_copy(q):
        k, first, wide = PIECES[q]
        return pltpu.make_async_copy(
            legendre_hbm.at[k, :, pl.ds(pl.multiple_of(me * degrees + first, 128), wide)],
            blocks.at[k, own_rows, pl.ds(first, wide)],
            block_recv.at[q],
        )

    def block_copy(q, i):
        k, first, wide = PIECES[q]
        dy, dx, dc = STEPS[i]
        there = chip_at(dy, dx) * CORES + (core + dc) % CORES
        return pltpu.make_async_remote_copy(
            src_ref=legendre_hbm.at[k, :, pl.ds(pl.multiple_of(there * degrees + first, 128), wide)],
            dst_ref=blocks.at[
                k, pl.ds(pl.multiple_of((1 - dc) * half + chip * rows, rows), rows), pl.ds(first, wide)
            ],
            send_sem=block_send.at[0],
            recv_sem=block_recv.at[q],
            device_id={"blk": there},
            device_id_type=MESH,
        )

    for load in loads[:4]:
        load.wait()
    row = lax.broadcasted_iota(jnp.int32, (rows, rows), 0)
    lane = lax.broadcasted_iota(jnp.int32, (rows, rows), 1)
    weight = jnp.sum(jnp.where(row == lane, own_weight[...], 0.0), axis=1, keepdims=True)
    for k in range(M):
        clusters = hits.shape[1]
        cycle = me * rows + lax.broadcasted_iota(jnp.int32, (rows, clusters), 0)
        hit = (cycle == hits[k : k + 1, :]).astype(F32)
        added = lax.dot_general(
            hit, flux[k], (((1,), (0,)), ((), ())), precision=lax.Precision.HIGHEST, preferred_element_type=F32
        )
        injected[k, own_rows, :] = weight * (own_cycles[k] + added)

    def inj_copy(ks, source, step, sem):
        place = injected.at[ks, pl.ds(pl.multiple_of(half + source * rows, rows), rows), :]
        return pltpu.make_async_remote_copy(
            src_ref=place,
            dst_ref=place,
            send_sem=inj_send.at[sem],
            recv_sem=inj_recv.at[sem],
            device_id=at(*step, 0),
            device_id_type=MESH,
        )

    inj_direct = [inj_copy(pl.ds(0, M), chip, step, 0) for step in RELAYS]
    inj_relayed = [inj_copy(0, chip_at(0, 1), step, 1) for step in RELAYS[1:]]
    inj_relayed += [inj_copy(1, chip_at(*step), RELAYS[0], 1) for step in RELAYS[1:]]

    pl.semaphore_wait(barrier, N - 1)
    for copy in inj_direct:
        copy.start()
    for i in range(N - 1):
        block_copy(0, i).start()
    own_copy(0).start()

    loads[4].wait()
    loads[5].wait()
    degree = me * degrees + lax.broadcasted_iota(jnp.int32, (1, degrees), 1)
    squares = jnp.sum(filters[...] * filters[...], axis=1)
    scale_of = (lax.broadcasted_iota(jnp.int32, (S, 128), 1) // SIMS) % S == lax.broadcasted_iota(jnp.int32, (S, 128), 0)
    for k in range(M):
        factor = jnp.where(degree >= order_ref[k], 2.0 * degree.astype(F32) + 1.0, 0.0)
        response = jnp.sum(squares * factor, axis=1, keepdims=True)
        responses[CHIPS + chip, k : k + 1, :] = jnp.sum(jnp.where(scale_of, response, 0.0), axis=0, keepdims=True)

    resp_copies = [
        pltpu.make_async_remote_copy(
            src_ref=responses.at[CHIPS + chip],
            dst_ref=responses.at[CHIPS + chip],
            send_sem=resp_send.at[0],
            recv_sem=resp_recv.at[0],
            device_id=at(dy, dx, 0),
            device_id_type=MESH,
        )
        for dy, dx in CHIP_STEPS
    ]
    for copy in resp_copies:
        copy.start()
    take(injected.at[:, pl.ds(0, 4 * rows), :], inj_recv.at[0])
    for copy in inj_relayed:
        copy.start()
    for q in range(1, len(PIECES)):
        for i in range(N - 1):
            block_copy(q, i).start()
        own_copy(q).start()

    total[...] = jnp.zeros_like(total)
    take(injected.at[:, pl.ds(0, 3 * rows), :], inj_recv.at[1])
    take(responses.at[pl.ds(0, CHIPS - 1)], resp_recv.at[0])
    pairs = [
        pltpu.make_async_remote_copy(
            src_ref=source,
            dst_ref=target,
            send_sem=pair_sem.at[i, 0],
            recv_sem=pair_sem.at[i, 1],
            device_id=at(0, 0, 1),
            device_id_type=MESH,
        )
        for i, (source, target) in enumerate(
            (
                (injected.at[:, pl.ds(half, half), :], injected.at[:, pl.ds(0, half), :]),
                (responses.at[pl.ds(CHIPS, CHIPS)], responses.at[pl.ds(0, CHIPS)]),
            )
        )
    ]
    for copy in pairs:
        copy.start()
    for copy in pairs:
        copy.wait_recv()
    for k in range(M):
        turned = jnp.transpose(injected[k])
        turned_high, turned_low = halves(turned)
        injected_t[k, 0:128, :] = turned_high
        injected_t[k, 128:256, :] = turned_low

    def core_copy(k):
        return pltpu.make_async_remote_copy(
            src_ref=total.at[k, pl.ds(0, half), :],
            dst_ref=from_core.at[k],
            send_sem=core_send.at[k],
            recv_sem=core_recv.at[k],
            device_id=at(0, 0, 1),
            device_id_type=MESH,
        )

    def sum_copy(k, i):
        dy, dx = CHIP_STEPS[i]
        return pltpu.make_async_remote_copy(
            src_ref=outgoing.at[k, i],
            dst_ref=arriving.at[k, i],
            send_sem=sum_send.at[k],
            recv_sem=sum_recv.at[k],
            device_id=at(dy, dx, 0),
            device_id_type=MESH,
        )

    def send_sums(k):
        core_copy(k).wait_recv()
        for i, (dy, dx) in enumerate(CHIP_STEPS):
            there = chip_at(dy, dx) * rows
            outgoing[k, i] = (
                total[k, pl.ds(pl.multiple_of(half + there, rows), rows), :]
                + from_core[k, pl.ds(pl.multiple_of(there, rows), rows), :]
            )
        kept[k] = total[k, own_rows, :] + from_core[k, pl.ds(pl.multiple_of(chip * rows, rows), rows), :]
        for i in range(CHIPS - 1):
            sum_copy(k, i).start()

    def take_sums(k):
        value = kept[k]
        take(arriving.at[k], sum_recv.at[k])
        for i in range(CHIPS - 1):
            value = value + arriving[k, i]
        out_ref[k] = value * scale[k : k + 1, :]

    parts = degrees // WIDE

    def part_of(n, carry):
        k = n // parts
        for q, (slot, first, wide) in enumerate(PIECES):

            @pl.when(n == slot * parts + first // WIDE)
            def _():
                take(blocks.at[slot, :, pl.ds(first, wide)], block_recv.at[q])

        start = pl.multiple_of((n % parts) * WIDE, WIDE)
        degree = me * degrees + start + lax.broadcasted_iota(jnp.int32, (1, WIDE), 1)
        block_high, block_low = halves(blocks[k, :, pl.ds(start, WIDE)])
        high[...] = block_high
        low[...] = block_low
        value = None
        for h in range(2):
            span = pl.ds(h * half, half)
            first = dot(injected_t[k, :, span], high[span, :])
            second = dot(injected_t[k, 0:128, span], low[span, :])
            term = first[0:128] + first[128:256] + second
            value = term if h == 0 else value + term
        harmonics[...] = jnp.where(degree >= order_ref[k], value, 0.0)
        for t in range(WIDE // 128):
            lanes = pl.ds(t * 128, 128)
            for s in range(S):
                sums = [None, None]
                for f in range(F):
                    row = filters[s, f : f + 1, pl.ds(start + t * 128, 128)]
                    for p in range(2):
                        term = row * harmonics[pl.ds((p * F + f) * SIMS, SIMS), lanes]
                        sums[p] = term if f == 0 else sums[p] + term
                for p in range(2):
                    out_high, out_low = halves(sums[p])
                    matched[pl.ds((p * S + s) * SIMS, SIMS), lanes] = out_high
                    matched[pl.ds(128 + (p * S + s) * SIMS, SIMS), lanes] = out_low
        for part in range(2):
            span = pl.ds(part * half, half)
            both = dot(high[span, :], matched[...], ((1,), (1,)))
            third = dot(low[span, :], matched[0:128], ((1,), (1,)))
            total[k, span, :] += both[:, 0:128] + both[:, 128:256] + third
            if part == 0:

                @pl.when(n % parts == parts - 1)
                def _():
                    core_copy(k).start()

        @pl.when(n == parts)
        def _():
            send_sums(0)

        return carry

    lax.fori_loop(0, M * parts, part_of, 0)

    send_sums(1)
    scale = L / jnp.sqrt(jnp.sum(responses[...], axis=0))
    take_sums(0)
    take_sums(1)

    take(injected.at[:, pl.ds(0, 4 * rows), :], inj_send.at[0])
    take(injected.at[:, pl.ds(0, 3 * rows), :], inj_send.at[1])
    take(responses.at[pl.ds(0, CHIPS - 1)], resp_send.at[0])
    for copy in pairs:
        copy.wait_send()
    for k in range(M):
        core_copy(k).wait_send()
        take(outgoing.at[k], sum_send.at[k])
    take(blocks.at[:, pl.ds(0, (N - 1) * rows), :], block_send.at[0])


def body(cycles, legendre, weight, filters, hits, flux, order):
    orders, rows, width = cycles.shape
    degrees = filters.shape[0]
    clusters = hits.shape[1]
    everyone = N * rows
    dma = pltpu.SemaphoreType.DMA
    anywhere = pl.BlockSpec(memory_space=pl.ANY)
    return pl.pallas_call(
        kernel,
        out_shape=pltpu.VMEM(cycles.shape, F32),
        in_specs=[anywhere] * 7,
        out_specs=pl.BlockSpec(memory_space=pltpu.VMEM),
        scratch_shapes=[
            pltpu.SMEM((orders,), jnp.int32),
            pltpu.VMEM((orders, rows, width), F32),
            pltpu.VMEM((1, rows), F32),
            pltpu.VMEM((S, F, degrees), F32),
            pltpu.VMEM((orders, clusters), jnp.int32),
            pltpu.VMEM((orders, clusters, width), F32),
            dma((6,)),
            pltpu.VMEM((orders, everyone, width), F32),
            pltpu.VMEM((orders, 2 * width, everyone), BF16),
            dma((2,)),
            dma((2,)),
            dma((2, 2)),
            pltpu.VMEM((N, orders, width), F32),
            dma((1,)),
            dma((1,)),
            pltpu.VMEM((orders, everyone, degrees), F32),
            dma((1,)),
            dma((len(PIECES),)),
            pltpu.VMEM((everyone, WIDE), BF16),
            pltpu.VMEM((everyone, WIDE), BF16),
            pltpu.VMEM((width, WIDE), F32),
            pltpu.VMEM((2 * width, WIDE), BF16),
            pltpu.VMEM((orders, everyone, width), F32),
            pltpu.VMEM((orders, everyone // 2, width), F32),
            dma((orders,)),
            dma((orders,)),
            pltpu.VMEM((orders, CHIPS - 1, rows, width), F32),
            pltpu.VMEM((orders, CHIPS - 1, rows, width), F32),
            pltpu.VMEM((orders, rows, width), F32),
            dma((orders,)),
            dma((orders,)),
        ],
        compiler_params=pltpu.CompilerParams(
            collective_id=0, has_side_effects=True, vmem_limit_bytes=60 * 1024 * 1024
        ),
    )(cycles, legendre, weight.reshape(1, rows), jnp.transpose(filters, (1, 2, 0)), hits, flux, order)


def solution(mesh):
    return jax.shard_map(
        body,
        mesh=mesh,
        in_specs=(
            P("order", "blk", None),
            P("order", "blk", None),
            P("blk"),
            P("blk", None, None),
            P("order", None),
            P("order", None, None),
            P("order"),
        ),
        out_specs=P("order", "blk", None),
        check_vma=False,
    )
```

```python
import functools

import jax
import jax.numpy as jnp
from jax import lax
from jax.experimental import pallas as pl
from jax.experimental.pallas import tpu as pltpu
from jax.sharding import PartitionSpec as P

L = 12288
F = 8
S = 8
SIMS = 8
M = 2
Y, X, CORES = 4, 2, 2
CHIPS = Y * X
N = CHIPS * CORES
WIDE = 256
SPLIT = 2
PIECES = ((0, 0, 768), (1, 0, 512), (1, 512, 256))

MESH = pl.DeviceIdType.MESH
F32 = jnp.float32
BF16 = jnp.bfloat16

CHIP_STEPS = ((2, 1), (2, 0), (1, 1), (3, 1), (0, 1), (1, 0), (3, 0))
PLACE = {step: i for i, step in enumerate(CHIP_STEPS + ((0, 0),))}
RELAYS = ((0, 1), (2, 0), (1, 0), (3, 0))
STEPS = tuple((dy, dx, dc) for dy, dx in CHIP_STEPS for dc in range(CORES)) + ((0, 0, 1),)


def back(dy, dx):
    return (Y - dy) % Y, dx


def halves(value):
    high = value.astype(BF16)
    return high, (value - high.astype(F32)).astype(BF16)


def take(ref, sem):
    pltpu.make_async_copy(ref, ref, sem).wait()


def dot(a, b, dims=((1,), (0,))):
    return lax.dot_general(a, b, (dims, ((), ())), preferred_element_type=F32)


def kernel(
    cycles_hbm, legendre_hbm, weight_hbm, filter_hbm, hit_hbm, flux_hbm, order_hbm, out_ref,
    order_ref, own_cycles, own_weight, filters, hits, flux, load_sem,
    injected, injected_t, inj_send, inj_recv, pair_sem,
    responses, resp_send, resp_recv,
    blocks, block_send, block_recv,
    high, low, harmonics, matched, total, from_core, core_send, core_recv, outgoing, arriving, kept, sum_send, sum_recv,
):
    me = lax.axis_index("blk")
    y, x, core = me // (X * CORES), (me // CORES) % X, me % CORES
    rows = own_cycles.shape[1]
    half = CHIPS * rows
    degrees = filters.shape[2]

    def chip_at(dy, dx):
        return ((y + dy) % Y) * X + (x + dx) % X

    def at(dy, dx, dc):
        return {"blk": chip_at(dy, dx) * CORES + (core + dc) % CORES}

    barrier = pltpu.get_barrier_semaphore()
    for step in STEPS:
        pl.semaphore_signal(barrier, inc=1, device_id=at(*step), device_id_type=MESH)

    loads = [
        pltpu.make_async_copy(source, target, load_sem.at[i])
        for i, (source, target) in enumerate(
            ((cycles_hbm, own_cycles), (weight_hbm, own_weight), (hit_hbm, hits), (flux_hbm, flux), (filter_hbm, filters), (order_hbm, order_ref))
        )
    ]
    for load in loads:
        load.start()

    def rows_of(step, same_core=1):
        return pl.ds(same_core * half + PLACE[step] * rows, rows)

    own_rows = rows_of((0, 0))

    def own_copy(q):
        k, first, wide = PIECES[q]
        return pltpu.make_async_copy(
            legendre_hbm.at[k, :, pl.ds(pl.multiple_of(me * degrees + first, 128), wide)],
            blocks.at[k, own_rows, pl.ds(first, wide)],
            block_recv.at[q],
        )

    def block_copy(q, i):
        k, first, wide = PIECES[q]
        dy, dx, dc = STEPS[i]
        there = chip_at(dy, dx) * CORES + (core + dc) % CORES
        return pltpu.make_async_remote_copy(
            src_ref=legendre_hbm.at[k, :, pl.ds(pl.multiple_of(there * degrees + first, 128), wide)],
            dst_ref=blocks.at[
                k, rows_of(back(dy, dx), 1 - dc), pl.ds(first, wide)
            ],
            send_sem=block_send.at[0],
            recv_sem=block_recv.at[q],
            device_id={"blk": there},
            device_id_type=MESH,
        )

    for load in loads[:4]:
        load.wait()
    row = lax.broadcasted_iota(jnp.int32, (rows, rows), 0)
    lane = lax.broadcasted_iota(jnp.int32, (rows, rows), 1)
    weight = jnp.sum(jnp.where(row == lane, own_weight[...], 0.0), axis=1, keepdims=True)
    for k in range(M):
        clusters = hits.shape[1]
        cycle = me * rows + lax.broadcasted_iota(jnp.int32, (rows, clusters), 0)
        hit = (cycle == hits[k : k + 1, :]).astype(F32)
        added = lax.dot_general(
            hit, flux[k], (((1,), (0,)), ((), ())), precision=lax.Precision.HIGHEST, preferred_element_type=F32
        )
        injected[k, own_rows, :] = weight * (own_cycles[k] + added)

    def inj_copy(ks, source, step, sem):
        seen = ((source[0] - step[0]) % Y, (source[1] - step[1]) % X)
        return pltpu.make_async_remote_copy(
            src_ref=injected.at[ks, rows_of(source), :],
            dst_ref=injected.at[ks, rows_of(seen), :],
            send_sem=inj_send.at[sem],
            recv_sem=inj_recv.at[sem],
            device_id=at(*step, 0),
            device_id_type=MESH,
        )

    inj_direct = [inj_copy(pl.ds(0, M), (0, 0), step, 0) for step in RELAYS]
    inj_relayed = [inj_copy(0, RELAYS[0], step, 1) for step in RELAYS[1:]]
    inj_relayed += [inj_copy(1, step, RELAYS[0], 1) for step in RELAYS[1:]]

    pl.semaphore_wait(barrier, N - 1)
    for copy in inj_direct:
        copy.start()
    for i in range(N - 1):
        block_copy(0, i).start()
    own_copy(0).start()

    loads[4].wait()
    loads[5].wait()
    degree = me * degrees + lax.broadcasted_iota(jnp.int32, (1, degrees), 1)
    squares = jnp.sum(filters[...] * filters[...], axis=1)
    scale_of = (lax.broadcasted_iota(jnp.int32, (S, 128), 1) // SIMS) % S == lax.broadcasted_iota(jnp.int32, (S, 128), 0)
    for k in range(M):
        factor = jnp.where(degree >= order_ref[k], 2.0 * degree.astype(F32) + 1.0, 0.0)
        response = jnp.sum(squares * factor, axis=1, keepdims=True)
        responses[N - 1, k : k + 1, :] = jnp.sum(jnp.where(scale_of, response, 0.0), axis=0, keepdims=True)

    resp_copies = [
        pltpu.make_async_remote_copy(
            src_ref=responses.at[N - 1],
            dst_ref=responses.at[CHIPS + PLACE[back(dy, dx)]],
            send_sem=resp_send.at[0],
            recv_sem=resp_recv.at[0],
            device_id=at(dy, dx, 0),
            device_id_type=MESH,
        )
        for dy, dx in CHIP_STEPS
    ]
    for copy in resp_copies:
        copy.start()
    take(injected.at[:, pl.ds(0, 4 * rows), :], inj_recv.at[0])
    for copy in inj_relayed:
        copy.start()
    for q in range(1, len(PIECES)):
        for i in range(N - 1):
            block_copy(q, i).start()
        own_copy(q).start()

    total[...] = jnp.zeros_like(total)
    take(injected.at[:, pl.ds(0, 3 * rows), :], inj_recv.at[1])
    take(responses.at[pl.ds(0, CHIPS - 1)], resp_recv.at[0])
    pairs = [
        pltpu.make_async_remote_copy(
            src_ref=source,
            dst_ref=target,
            send_sem=pair_sem.at[i, 0],
            recv_sem=pair_sem.at[i, 1],
            device_id=at(0, 0, 1),
            device_id_type=MESH,
        )
        for i, (source, target) in enumerate(
            (
                (injected.at[:, pl.ds(half, half), :], injected.at[:, pl.ds(0, half), :]),
                (responses.at[pl.ds(CHIPS, CHIPS)], responses.at[pl.ds(0, CHIPS)]),
            )
        )
    ]
    for copy in pairs:
        copy.start()
    for copy in pairs:
        copy.wait_recv()
    for k in range(M):
        turned = jnp.transpose(injected[k])
        turned_high, turned_low = halves(turned)
        injected_t[k, 0:128, :] = turned_high
        injected_t[k, 128:256, :] = turned_low

    def core_copy(k, piece):
        place = pl.ds(piece * half // SPLIT, half // SPLIT)
        return pltpu.make_async_remote_copy(
            src_ref=total.at[k, place, :],
            dst_ref=from_core.at[k, place, :],
            send_sem=core_send.at[k],
            recv_sem=core_recv.at[k],
            device_id=at(0, 0, 1),
            device_id_type=MESH,
        )

    def sum_copy(k, i):
        dy, dx = CHIP_STEPS[i]
        return pltpu.make_async_remote_copy(
            src_ref=outgoing.at[k, pl.ds(i * rows, rows), :],
            dst_ref=arriving.at[k, i],
            send_sem=sum_send.at[k],
            recv_sem=sum_recv.at[k],
            device_id=at(dy, dx, 0),
            device_id_type=MESH,
        )

    def send_sums(k):
        take(from_core.at[k], core_recv.at[k])
        others = (CHIPS - 1) * rows
        outgoing[k] = total[k, pl.ds(half, others), :] + from_core[k, pl.ds(0, others), :]
        kept[k] = total[k, own_rows, :] + from_core[k, pl.ds(others, rows), :]
        for i in range(CHIPS - 1):
            sum_copy(k, i).start()

    def take_sums(k):
        value = kept[k]
        take(arriving.at[k], sum_recv.at[k])
        for i in range(CHIPS - 1):
            value = value + arriving[k, i]
        out_ref[k] = value * scale[k : k + 1, :]

    parts = degrees // WIDE

    def part_of(n, carry):
        k = n // parts
        for q, (slot, first, wide) in enumerate(PIECES):

            @pl.when(n == slot * parts + first // WIDE)
            def _():
                take(blocks.at[slot, :, pl.ds(first, wide)], block_recv.at[q])

        start = pl.multiple_of((n % parts) * WIDE, WIDE)
        degree = me * degrees + start + lax.broadcasted_iota(jnp.int32, (1, WIDE), 1)
        block_high, block_low = halves(blocks[k, :, pl.ds(start, WIDE)])
        high[...] = block_high
        low[...] = block_low
        value = None
        for h in range(2):
            span = pl.ds(h * half, half)
            first = dot(injected_t[k, :, span], high[span, :])
            second = dot(injected_t[k, 0:128, span], low[span, :])
            term = first[0:128] + first[128:256] + second
            value = term if h == 0 else value + term
        harmonics[...] = jnp.where(degree >= order_ref[k], value, 0.0)
        for t in range(WIDE // 128):
            lanes = pl.ds(t * 128, 128)
            for s in range(S):
                sums = [None, None]
                for f in range(F):
                    row = filters[s, f : f + 1, pl.ds(start + t * 128, 128)]
                    for p in range(2):
                        term = row * harmonics[pl.ds((p * F + f) * SIMS, SIMS), lanes]
                        sums[p] = term if f == 0 else sums[p] + term
                for p in range(2):
                    out_high, out_low = halves(sums[p])
                    matched[pl.ds((p * S + s) * SIMS, SIMS), lanes] = out_high
                    matched[pl.ds(128 + (p * S + s) * SIMS, SIMS), lanes] = out_low
        for part in range(2):
            span = pl.ds(part * half, half)
            both = dot(high[span, :], matched[...], ((1,), (1,)))
            third = dot(low[span, :], matched[0:128], ((1,), (1,)))
            total[k, span, :] += both[:, 0:128] + both[:, 128:256] + third
            if part == 0:

                @pl.when(n % parts == parts - 1)
                def _():
                    for piece in range(SPLIT):
                        core_copy(k, piece).start()

        @pl.when(n == parts)
        def _():
            send_sums(0)

        return carry

    lax.fori_loop(0, M * parts, part_of, 0)

    send_sums(1)
    scale = L / jnp.sqrt(jnp.sum(responses[...], axis=0))
    take_sums(0)
    take_sums(1)

    take(injected.at[:, pl.ds(0, 4 * rows), :], inj_send.at[0])
    take(injected.at[:, pl.ds(0, 3 * rows), :], inj_send.at[1])
    take(responses.at[pl.ds(0, CHIPS - 1)], resp_send.at[0])
    for copy in pairs:
        copy.wait_send()
    for k in range(M):
        take(from_core.at[k], core_send.at[k])
        take(outgoing.at[k], sum_send.at[k])
    take(blocks.at[:, pl.ds(0, (N - 1) * rows), :], block_send.at[0])


def body(cycles, legendre, weight, filters, hits, flux, order):
    orders, rows, width = cycles.shape
    degrees = filters.shape[0]
    clusters = hits.shape[1]
    everyone = N * rows
    dma = pltpu.SemaphoreType.DMA
    anywhere = pl.BlockSpec(memory_space=pl.ANY)
    return pl.pallas_call(
        kernel,
        out_shape=pltpu.VMEM(cycles.shape, F32),
        in_specs=[anywhere] * 7,
        out_specs=pl.BlockSpec(memory_space=pltpu.VMEM),
        scratch_shapes=[
            pltpu.SMEM((orders,), jnp.int32),
            pltpu.VMEM((orders, rows, width), F32),
            pltpu.VMEM((1, rows), F32),
            pltpu.VMEM((S, F, degrees), F32),
            pltpu.VMEM((orders, clusters), jnp.int32),
            pltpu.VMEM((orders, clusters, width), F32),
            dma((6,)),
            pltpu.VMEM((orders, everyone, width), F32),
            pltpu.VMEM((orders, 2 * width, everyone), BF16),
            dma((2,)),
            dma((2,)),
            dma((2, 2)),
            pltpu.VMEM((N, orders, width), F32),
            dma((1,)),
            dma((1,)),
            pltpu.VMEM((orders, everyone, degrees), F32),
            dma((1,)),
            dma((len(PIECES),)),
            pltpu.VMEM((everyone, WIDE), BF16),
            pltpu.VMEM((everyone, WIDE), BF16),
            pltpu.VMEM((width, WIDE), F32),
            pltpu.VMEM((2 * width, WIDE), BF16),
            pltpu.VMEM((orders, everyone, width), F32),
            pltpu.VMEM((orders, everyone // 2, width), F32),
            dma((orders,)),
            dma((orders,)),
            pltpu.VMEM((orders, (CHIPS - 1) * rows, width), F32),
            pltpu.VMEM((orders, CHIPS - 1, rows, width), F32),
            pltpu.VMEM((orders, rows, width), F32),
            dma((orders,)),
            dma((orders,)),
        ],
        compiler_params=pltpu.CompilerParams(
            collective_id=0, has_side_effects=True, vmem_limit_bytes=60 * 1024 * 1024
        ),
    )(cycles, legendre, weight.reshape(1, rows), jnp.transpose(filters, (1, 2, 0)), hits, flux, order)


def solution(mesh):
    return jax.shard_map(
        body,
        mesh=mesh,
        in_specs=(
            P("order", "blk", None),
            P("order", "blk", None),
            P("blk"),
            P("blk", None, None),
            P("order", None),
            P("order", None, None),
            P("order"),
        ),
        out_specs=P("order", "blk", None),
        check_vma=False,
    )
```

```python
import functools

import jax
import jax.numpy as jnp
from jax import lax
from jax.experimental import pallas as pl
from jax.experimental.pallas import tpu as pltpu
from jax.sharding import PartitionSpec as P

L = 12288
F = 8
S = 8
SIMS = 8
M = 2
Y, X, CORES = 4, 2, 2
CHIPS = Y * X
N = CHIPS * CORES
WIDE = 256
SPLIT = 2
PIECES = ((0, 0, 768), (1, 0, 512), (1, 512, 256))

MESH = pl.DeviceIdType.MESH
F32 = jnp.float32
BF16 = jnp.bfloat16

CHIP_STEPS = ((2, 1), (2, 0), (1, 1), (3, 1), (0, 1), (1, 0), (3, 0))
PLACE = {step: i for i, step in enumerate(CHIP_STEPS + ((0, 0),))}
RELAYS = ((0, 1), (2, 0), (1, 0), (3, 0))
STEPS = tuple((dy, dx, dc) for dy, dx in CHIP_STEPS for dc in range(CORES)) + ((0, 0, 1),)


def back(dy, dx):
    return (Y - dy) % Y, dx


def halves(value):
    high = value.astype(BF16)
    return high, (value - high.astype(F32)).astype(BF16)


def take(ref, sem):
    pltpu.make_async_copy(ref, ref, sem).wait()


def dot(a, b, dims=((1,), (0,))):
    return lax.dot_general(a, b, (dims, ((), ())), preferred_element_type=F32)


def kernel(
    cycles_hbm, legendre_hbm, weight_hbm, filter_hbm, hit_hbm, flux_hbm, order_hbm, out_ref,
    order_ref, own_cycles, own_weight, filters, hits, flux, load_sem,
    injected, injected_t, inj_send, inj_recv, pair_sem,
    responses, resp_send, resp_recv,
    blocks, block_send, block_recv,
    high, low, harmonics, matched, total, from_core, core_send, core_recv, outgoing, arriving, kept, sum_send, sum_recv,
):
    me = lax.axis_index("blk")
    y, x, core = me // (X * CORES), (me // CORES) % X, me % CORES
    rows = own_cycles.shape[1]
    half = CHIPS * rows
    degrees = filters.shape[2]

    def chip_at(dy, dx):
        return ((y + dy) % Y) * X + (x + dx) % X

    def at(dy, dx, dc):
        return {"blk": chip_at(dy, dx) * CORES + (core + dc) % CORES}

    barrier = pltpu.get_barrier_semaphore()
    for step in STEPS:
        pl.semaphore_signal(barrier, inc=1, device_id=at(*step), device_id_type=MESH)

    loads = [
        pltpu.make_async_copy(source, target, load_sem.at[i])
        for i, (source, target) in enumerate(
            ((cycles_hbm, own_cycles), (weight_hbm, own_weight), (hit_hbm, hits), (flux_hbm, flux), (filter_hbm, filters), (order_hbm, order_ref))
        )
    ]
    for load in loads:
        load.start()

    def rows_of(step, same_core=1):
        return pl.ds(same_core * half + PLACE[step] * rows, rows)

    own_rows = rows_of((0, 0))

    def own_copy(q):
        k, first, wide = PIECES[q]
        return pltpu.make_async_copy(
            legendre_hbm.at[k, :, pl.ds(pl.multiple_of(me * degrees + first, 128), wide)],
            blocks.at[k, own_rows, pl.ds(first, wide)],
            block_recv.at[q],
        )

    def block_copy(q, i):
        k, first, wide = PIECES[q]
        dy, dx, dc = STEPS[i]
        there = chip_at(dy, dx) * CORES + (core + dc) % CORES
        return pltpu.make_async_remote_copy(
            src_ref=legendre_hbm.at[k, :, pl.ds(pl.multiple_of(there * degrees + first, 128), wide)],
            dst_ref=blocks.at[
                k, rows_of(back(dy, dx), 1 - dc), pl.ds(first, wide)
            ],
            send_sem=block_send.at[0],
            recv_sem=block_recv.at[q],
            device_id={"blk": there},
            device_id_type=MESH,
        )

    for load in loads[:4]:
        load.wait()
    row = lax.broadcasted_iota(jnp.int32, (rows, rows), 0)
    lane = lax.broadcasted_iota(jnp.int32, (rows, rows), 1)
    weight = jnp.sum(jnp.where(row == lane, own_weight[...], 0.0), axis=1, keepdims=True)
    for k in range(M):
        clusters = hits.shape[1]
        cycle = me * rows + lax.broadcasted_iota(jnp.int32, (rows, clusters), 0)
        hit = (cycle == hits[k : k + 1, :]).astype(F32)
        added = lax.dot_general(
            hit, flux[k], (((1,), (0,)), ((), ())), precision=lax.Precision.HIGHEST, preferred_element_type=F32
        )
        injected[k, own_rows, :] = weight * (own_cycles[k] + added)

    def inj_copy(ks, source, step, sem):
        seen = ((source[0] - step[0]) % Y, (source[1] - step[1]) % X)
        return pltpu.make_async_remote_copy(
            src_ref=injected.at[ks, rows_of(source), :],
            dst_ref=injected.at[ks, rows_of(seen), :],
            send_sem=inj_send.at[sem],
            recv_sem=inj_recv.at[sem],
            device_id=at(*step, 0),
            device_id_type=MESH,
        )

    inj_direct = [inj_copy(pl.ds(0, M), (0, 0), step, 0) for step in RELAYS]
    inj_relayed = [inj_copy(0, RELAYS[0], step, 1) for step in RELAYS[1:]]
    inj_relayed += [inj_copy(1, step, RELAYS[0], 1) for step in RELAYS[1:]]

    pl.semaphore_wait(barrier, N - 1)
    for copy in inj_direct:
        copy.start()
    for i in range(N - 1):
        block_copy(0, i).start()
    own_copy(0).start()

    loads[4].wait()
    loads[5].wait()
    degree = me * degrees + lax.broadcasted_iota(jnp.int32, (1, degrees), 1)
    squares = jnp.sum(filters[...] * filters[...], axis=1)
    scale_of = (lax.broadcasted_iota(jnp.int32, (S, 128), 1) // SIMS) % S == lax.broadcasted_iota(jnp.int32, (S, 128), 0)
    for k in range(M):
        factor = jnp.where(degree >= order_ref[k], 2.0 * degree.astype(F32) + 1.0, 0.0)
        response = jnp.sum(squares * factor, axis=1, keepdims=True)
        responses[N - 1, k : k + 1, :] = jnp.sum(jnp.where(scale_of, response, 0.0), axis=0, keepdims=True)

    resp_copies = [
        pltpu.make_async_remote_copy(
            src_ref=responses.at[N - 1],
            dst_ref=responses.at[CHIPS + PLACE[back(dy, dx)]],
            send_sem=resp_send.at[0],
            recv_sem=resp_recv.at[0],
            device_id=at(dy, dx, 0),
            device_id_type=MESH,
        )
        for dy, dx in CHIP_STEPS
    ]
    for copy in resp_copies:
        copy.start()
    take(injected.at[:, pl.ds(0, 4 * rows), :], inj_recv.at[0])
    for copy in inj_relayed:
        copy.start()
    for q in range(1, len(PIECES)):
        for i in range(N - 1):
            block_copy(q, i).start()
        own_copy(q).start()

    total[...] = jnp.zeros_like(total)
    take(injected.at[:, pl.ds(0, 3 * rows), :], inj_recv.at[1])
    take(responses.at[pl.ds(0, CHIPS - 1)], resp_recv.at[0])
    pairs = [
        pltpu.make_async_remote_copy(
            src_ref=source,
            dst_ref=target,
            send_sem=pair_sem.at[i, 0],
            recv_sem=pair_sem.at[i, 1],
            device_id=at(0, 0, 1),
            device_id_type=MESH,
        )
        for i, (source, target) in enumerate(
            (
                (injected.at[:, pl.ds(half, half), :], injected.at[:, pl.ds(0, half), :]),
                (responses.at[pl.ds(CHIPS, CHIPS)], responses.at[pl.ds(0, CHIPS)]),
            )
        )
    ]
    for copy in pairs:
        copy.start()
    for copy in pairs:
        copy.wait_recv()
    for k in range(M):
        turned = jnp.transpose(injected[k])
        turned_high, turned_low = halves(turned)
        injected_t[k, 0:128, :] = turned_high
        injected_t[k, 128:256, :] = turned_low

    def core_copy(k, piece):
        place = pl.ds(piece * half // SPLIT, half // SPLIT)
        return pltpu.make_async_remote_copy(
            src_ref=total.at[k, place, :],
            dst_ref=from_core.at[k, place, :],
            send_sem=core_send.at[k],
            recv_sem=core_recv.at[k, piece],
            device_id=at(0, 0, 1),
            device_id_type=MESH,
        )

    def sum_copy(k, i):
        dy, dx = CHIP_STEPS[i]
        return pltpu.make_async_remote_copy(
            src_ref=outgoing.at[k, pl.ds(i * rows, rows), :],
            dst_ref=arriving.at[k, i],
            send_sem=sum_send.at[k],
            recv_sem=sum_recv.at[k],
            device_id=at(dy, dx, 0),
            device_id_type=MESH,
        )

    def send_sums(k):
        for piece in range(SPLIT):
            core_copy(k, piece).wait_recv()
            chips = range(piece * CHIPS // SPLIT, min((piece + 1) * CHIPS // SPLIT, CHIPS - 1))
            first, size = chips[0] * rows, len(chips) * rows
            outgoing[k, pl.ds(first, size), :] = (
                total[k, pl.ds(half + first, size), :] + from_core[k, pl.ds(first, size), :]
            )
            if piece == SPLIT - 1:
                kept[k] = total[k, own_rows, :] + from_core[k, pl.ds((CHIPS - 1) * rows, rows), :]
            for i in chips:
                sum_copy(k, i).start()

    def take_sums(k):
        value = kept[k]
        take(arriving.at[k], sum_recv.at[k])
        for i in range(CHIPS - 1):
            value = value + arriving[k, i]
        out_ref[k] = value * scale[k : k + 1, :]

    parts = degrees // WIDE

    def part_of(n, carry):
        k = n // parts
        for q, (slot, first, wide) in enumerate(PIECES):

            @pl.when(n == slot * parts + first // WIDE)
            def _():
                take(blocks.at[slot, :, pl.ds(first, wide)], block_recv.at[q])

        start = pl.multiple_of((n % parts) * WIDE, WIDE)
        degree = me * degrees + start + lax.broadcasted_iota(jnp.int32, (1, WIDE), 1)
        block_high, block_low = halves(blocks[k, :, pl.ds(start, WIDE)])
        high[...] = block_high
        low[...] = block_low
        value = None
        for h in range(2):
            span = pl.ds(h * half, half)
            first = dot(injected_t[k, :, span], high[span, :])
            second = dot(injected_t[k, 0:128, span], low[span, :])
            term = first[0:128] + first[128:256] + second
            value = term if h == 0 else value + term
        harmonics[...] = jnp.where(degree >= order_ref[k], value, 0.0)
        for t in range(WIDE // 128):
            lanes = pl.ds(t * 128, 128)
            for s in range(S):
                sums = [None, None]
                for f in range(F):
                    row = filters[s, f : f + 1, pl.ds(start + t * 128, 128)]
                    for p in range(2):
                        term = row * harmonics[pl.ds((p * F + f) * SIMS, SIMS), lanes]
                        sums[p] = term if f == 0 else sums[p] + term
                for p in range(2):
                    out_high, out_low = halves(sums[p])
                    matched[pl.ds((p * S + s) * SIMS, SIMS), lanes] = out_high
                    matched[pl.ds(128 + (p * S + s) * SIMS, SIMS), lanes] = out_low
        for part in range(2):
            span = pl.ds(part * half, half)
            both = dot(high[span, :], matched[...], ((1,), (1,)))
            third = dot(low[span, :], matched[0:128], ((1,), (1,)))
            total[k, span, :] += both[:, 0:128] + both[:, 128:256] + third
            if part == 0:

                @pl.when(n % parts == parts - 1)
                def _():
                    for piece in range(SPLIT):
                        core_copy(k, piece).start()

        @pl.when(n == parts)
        def _():
            send_sums(0)

        return carry

    lax.fori_loop(0, M * parts, part_of, 0)

    send_sums(1)
    scale = L / jnp.sqrt(jnp.sum(responses[...], axis=0))
    take_sums(0)
    take_sums(1)

    take(injected.at[:, pl.ds(0, 4 * rows), :], inj_send.at[0])
    take(injected.at[:, pl.ds(0, 3 * rows), :], inj_send.at[1])
    take(responses.at[pl.ds(0, CHIPS - 1)], resp_send.at[0])
    for copy in pairs:
        copy.wait_send()
    for k in range(M):
        take(from_core.at[k], core_send.at[k])
        take(outgoing.at[k], sum_send.at[k])
    take(blocks.at[:, pl.ds(0, (N - 1) * rows), :], block_send.at[0])


def body(cycles, legendre, weight, filters, hits, flux, order):
    orders, rows, width = cycles.shape
    degrees = filters.shape[0]
    clusters = hits.shape[1]
    everyone = N * rows
    dma = pltpu.SemaphoreType.DMA
    anywhere = pl.BlockSpec(memory_space=pl.ANY)
    return pl.pallas_call(
        kernel,
        out_shape=pltpu.VMEM(cycles.shape, F32),
        in_specs=[anywhere] * 7,
        out_specs=pl.BlockSpec(memory_space=pltpu.VMEM),
        scratch_shapes=[
            pltpu.SMEM((orders,), jnp.int32),
            pltpu.VMEM((orders, rows, width), F32),
            pltpu.VMEM((1, rows), F32),
            pltpu.VMEM((S, F, degrees), F32),
            pltpu.VMEM((orders, clusters), jnp.int32),
            pltpu.VMEM((orders, clusters, width), F32),
            dma((6,)),
            pltpu.VMEM((orders, everyone, width), F32),
            pltpu.VMEM((orders, 2 * width, everyone), BF16),
            dma((2,)),
            dma((2,)),
            dma((2, 2)),
            pltpu.VMEM((N, orders, width), F32),
            dma((1,)),
            dma((1,)),
            pltpu.VMEM((orders, everyone, degrees), F32),
            dma((1,)),
            dma((len(PIECES),)),
            pltpu.VMEM((everyone, WIDE), BF16),
            pltpu.VMEM((everyone, WIDE), BF16),
            pltpu.VMEM((width, WIDE), F32),
            pltpu.VMEM((2 * width, WIDE), BF16),
            pltpu.VMEM((orders, everyone, width), F32),
            pltpu.VMEM((orders, everyone // 2, width), F32),
            dma((orders,)),
            dma((orders, SPLIT)),
            pltpu.VMEM((orders, (CHIPS - 1) * rows, width), F32),
            pltpu.VMEM((orders, CHIPS - 1, rows, width), F32),
            pltpu.VMEM((orders, rows, width), F32),
            dma((orders,)),
            dma((orders,)),
        ],
        compiler_params=pltpu.CompilerParams(
            collective_id=0, has_side_effects=True, vmem_limit_bytes=60 * 1024 * 1024
        ),
    )(cycles, legendre, weight.reshape(1, rows), jnp.transpose(filters, (1, 2, 0)), hits, flux, order)


def solution(mesh):
    return jax.shard_map(
        body,
        mesh=mesh,
        in_specs=(
            P("order", "blk", None),
            P("order", "blk", None),
            P("blk"),
            P("blk", None, None),
            P("order", None),
            P("order", None, None),
            P("order"),
        ),
        out_specs=P("order", "blk", None),
        check_vma=False,
    )
```

```python
import functools

import jax
import jax.numpy as jnp
from jax import lax
from jax.experimental import pallas as pl
from jax.experimental.pallas import tpu as pltpu
from jax.sharding import PartitionSpec as P

L = 12288
F = 8
S = 8
SIMS = 8
M = 2
Y, X, CORES = 4, 2, 2
CHIPS = Y * X
N = CHIPS * CORES
WIDE = 256
SPLIT = 2
PIECES = ((0, 0, 768), (1, 0, 512), (1, 512, 256))

MESH = pl.DeviceIdType.MESH
F32 = jnp.float32
BF16 = jnp.bfloat16

CHIP_STEPS = ((2, 1), (2, 0), (1, 1), (3, 1), (0, 1), (1, 0), (3, 0))
PLACE = {step: i for i, step in enumerate(CHIP_STEPS + ((0, 0),))}
RELAYS = ((0, 1), (2, 0), (1, 0), (3, 0))
STEPS = tuple((dy, dx, dc) for dy, dx in CHIP_STEPS for dc in range(CORES)) + ((0, 0, 1),)


def back(dy, dx):
    return (Y - dy) % Y, dx


def halves(value):
    high = value.astype(BF16)
    return high, (value - high.astype(F32)).astype(BF16)


def take(ref, sem):
    pltpu.make_async_copy(ref, ref, sem).wait()


def dot(a, b, dims=((1,), (0,))):
    return lax.dot_general(a, b, (dims, ((), ())), preferred_element_type=F32)


def kernel(
    cycles_hbm, legendre_hbm, weight_hbm, filter_hbm, hit_hbm, flux_hbm, order_hbm, out_ref,
    order_ref, own_cycles, own_weight, filters, hits, flux, load_sem,
    injected, injected_t, inj_send, inj_recv, pair_sem,
    responses, resp_send, resp_recv,
    blocks, block_send, block_recv,
    high, low, harmonics, matched, total, from_core, core_send, core_recv, outgoing, arriving, kept, sum_send, sum_recv,
):
    me = lax.axis_index("blk")
    y, x, core = me // (X * CORES), (me // CORES) % X, me % CORES
    rows = own_cycles.shape[1]
    half = CHIPS * rows
    degrees = filters.shape[2]

    def chip_at(dy, dx):
        return ((y + dy) % Y) * X + (x + dx) % X

    def at(dy, dx, dc):
        return {"blk": chip_at(dy, dx) * CORES + (core + dc) % CORES}

    loads = [
        pltpu.make_async_copy(source, target, load_sem.at[i])
        for i, (source, target) in enumerate(
            ((cycles_hbm, own_cycles), (weight_hbm, own_weight), (hit_hbm, hits), (flux_hbm, flux), (filter_hbm, filters), (order_hbm, order_ref))
        )
    ]
    for load in loads:
        load.start()

    barrier = pltpu.get_barrier_semaphore()
    for step in STEPS:
        pl.semaphore_signal(barrier, inc=1, device_id=at(*step), device_id_type=MESH)

    def rows_of(step, same_core=1):
        return pl.ds(same_core * half + PLACE[step] * rows, rows)

    own_rows = rows_of((0, 0))

    def own_copy(q):
        k, first, wide = PIECES[q]
        return pltpu.make_async_copy(
            legendre_hbm.at[k, :, pl.ds(pl.multiple_of(me * degrees + first, 128), wide)],
            blocks.at[k, own_rows, pl.ds(first, wide)],
            block_recv.at[q],
        )

    def block_copy(q, i):
        k, first, wide = PIECES[q]
        dy, dx, dc = STEPS[i]
        there = chip_at(dy, dx) * CORES + (core + dc) % CORES
        return pltpu.make_async_remote_copy(
            src_ref=legendre_hbm.at[k, :, pl.ds(pl.multiple_of(there * degrees + first, 128), wide)],
            dst_ref=blocks.at[
                k, rows_of(back(dy, dx), 1 - dc), pl.ds(first, wide)
            ],
            send_sem=block_send.at[0],
            recv_sem=block_recv.at[q],
            device_id={"blk": there},
            device_id_type=MESH,
        )

    for load in loads[:4]:
        load.wait()
    row = lax.broadcasted_iota(jnp.int32, (rows, rows), 0)
    lane = lax.broadcasted_iota(jnp.int32, (rows, rows), 1)
    weight = jnp.sum(jnp.where(row == lane, own_weight[...], 0.0), axis=1, keepdims=True)
    for k in range(M):
        clusters = hits.shape[1]
        cycle = me * rows + lax.broadcasted_iota(jnp.int32, (rows, clusters), 0)
        hit = (cycle == hits[k : k + 1, :]).astype(F32)
        added = lax.dot_general(
            hit, flux[k], (((1,), (0,)), ((), ())), precision=lax.Precision.HIGHEST, preferred_element_type=F32
        )
        injected[k, own_rows, :] = weight * (own_cycles[k] + added)

    def inj_copy(ks, source, step, sem):
        seen = ((source[0] - step[0]) % Y, (source[1] - step[1]) % X)
        return pltpu.make_async_remote_copy(
            src_ref=injected.at[ks, rows_of(source), :],
            dst_ref=injected.at[ks, rows_of(seen), :],
            send_sem=inj_send.at[sem],
            recv_sem=inj_recv.at[sem],
            device_id=at(*step, 0),
            device_id_type=MESH,
        )

    inj_direct = [inj_copy(pl.ds(0, M), (0, 0), step, 0) for step in RELAYS]
    inj_relayed = [inj_copy(0, RELAYS[0], step, 1) for step in RELAYS[1:]]
    inj_relayed += [inj_copy(1, step, RELAYS[0], 1) for step in RELAYS[1:]]

    pl.semaphore_wait(barrier, N - 1)
    for copy in inj_direct:
        copy.start()
    for i in range(N - 1):
        block_copy(0, i).start()
    own_copy(0).start()

    loads[4].wait()
    loads[5].wait()
    degree = me * degrees + lax.broadcasted_iota(jnp.int32, (1, degrees), 1)
    squares = jnp.sum(filters[...] * filters[...], axis=1)
    scale_of = (lax.broadcasted_iota(jnp.int32, (S, 128), 1) // SIMS) % S == lax.broadcasted_iota(jnp.int32, (S, 128), 0)
    for k in range(M):
        factor = jnp.where(degree >= order_ref[k], 2.0 * degree.astype(F32) + 1.0, 0.0)
        response = jnp.sum(squares * factor, axis=1, keepdims=True)
        responses[N - 1, k : k + 1, :] = jnp.sum(jnp.where(scale_of, response, 0.0), axis=0, keepdims=True)

    resp_copies = [
        pltpu.make_async_remote_copy(
            src_ref=responses.at[N - 1],
            dst_ref=responses.at[CHIPS + PLACE[back(dy, dx)]],
            send_sem=resp_send.at[0],
            recv_sem=resp_recv.at[0],
            device_id=at(dy, dx, 0),
            device_id_type=MESH,
        )
        for dy, dx in CHIP_STEPS
    ]
    for copy in resp_copies:
        copy.start()
    take(injected.at[:, pl.ds(0, 4 * rows), :], inj_recv.at[0])
    for copy in inj_relayed:
        copy.start()
    for q in range(1, len(PIECES)):
        for i in range(N - 1):
            block_copy(q, i).start()
        own_copy(q).start()

    total[...] = jnp.zeros_like(total)
    take(injected.at[:, pl.ds(0, 3 * rows), :], inj_recv.at[1])
    take(responses.at[pl.ds(0, CHIPS - 1)], resp_recv.at[0])
    pairs = [
        pltpu.make_async_remote_copy(
            src_ref=source,
            dst_ref=target,
            send_sem=pair_sem.at[i, 0],
            recv_sem=pair_sem.at[i, 1],
            device_id=at(0, 0, 1),
            device_id_type=MESH,
        )
        for i, (source, target) in enumerate(
            (
                (injected.at[:, pl.ds(half, half), :], injected.at[:, pl.ds(0, half), :]),
                (responses.at[pl.ds(CHIPS, CHIPS)], responses.at[pl.ds(0, CHIPS)]),
            )
        )
    ]
    for copy in pairs:
        copy.start()
    for copy in pairs:
        copy.wait_recv()
    for k in range(M):
        turned = jnp.transpose(injected[k])
        turned_high, turned_low = halves(turned)
        injected_t[k, 0:128, :] = turned_high
        injected_t[k, 128:256, :] = turned_low

    def core_copy(k, piece):
        place = pl.ds(piece * half // SPLIT, half // SPLIT)
        return pltpu.make_async_remote_copy(
            src_ref=total.at[k, place, :],
            dst_ref=from_core.at[k, place, :],
            send_sem=core_send.at[k],
            recv_sem=core_recv.at[k],
            device_id=at(0, 0, 1),
            device_id_type=MESH,
        )

    def sum_copy(k, i):
        dy, dx = CHIP_STEPS[i]
        return pltpu.make_async_remote_copy(
            src_ref=outgoing.at[k, pl.ds(i * rows, rows), :],
            dst_ref=arriving.at[k, i],
            send_sem=sum_send.at[k],
            recv_sem=sum_recv.at[k],
            device_id=at(dy, dx, 0),
            device_id_type=MESH,
        )

    def send_sums(k):
        take(from_core.at[k], core_recv.at[k])
        others = (CHIPS - 1) * rows
        outgoing[k] = total[k, pl.ds(half, others), :] + from_core[k, pl.ds(0, others), :]
        kept[k] = total[k, own_rows, :] + from_core[k, pl.ds(others, rows), :]
        for i in range(CHIPS - 1):
            sum_copy(k, i).start()

    def take_sums(k):
        value = kept[k]
        take(arriving.at[k], sum_recv.at[k])
        for i in range(CHIPS - 1):
            value = value + arriving[k, i]
        out_ref[k] = value * scale[k : k + 1, :]

    parts = degrees // WIDE

    def part_of(n, carry):
        k = n // parts
        for q, (slot, first, wide) in enumerate(PIECES):

            @pl.when(n == slot * parts + first // WIDE)
            def _():
                take(blocks.at[slot, :, pl.ds(first, wide)], block_recv.at[q])

        start = pl.multiple_of((n % parts) * WIDE, WIDE)
        degree = me * degrees + start + lax.broadcasted_iota(jnp.int32, (1, WIDE), 1)
        block_high, block_low = halves(blocks[k, :, pl.ds(start, WIDE)])
        high[...] = block_high
        low[...] = block_low
        value = None
        for h in range(2):
            span = pl.ds(h * half, half)
            first = dot(injected_t[k, :, span], high[span, :])
            second = dot(injected_t[k, 0:128, span], low[span, :])
            term = first[0:128] + first[128:256] + second
            value = term if h == 0 else value + term
        harmonics[...] = jnp.where(degree >= order_ref[k], value, 0.0)
        for t in range(WIDE // 128):
            lanes = pl.ds(t * 128, 128)
            for s in range(S):
                sums = [None, None]
                for f in range(F):
                    row = filters[s, f : f + 1, pl.ds(start + t * 128, 128)]
                    for p in range(2):
                        term = row * harmonics[pl.ds((p * F + f) * SIMS, SIMS), lanes]
                        sums[p] = term if f == 0 else sums[p] + term
                for p in range(2):
                    out_high, out_low = halves(sums[p])
                    matched[pl.ds((p * S + s) * SIMS, SIMS), lanes] = out_high
                    matched[pl.ds(128 + (p * S + s) * SIMS, SIMS), lanes] = out_low
        for part in range(2):
            span = pl.ds(part * half, half)
            both = dot(high[span, :], matched[...], ((1,), (1,)))
            third = dot(low[span, :], matched[0:128], ((1,), (1,)))
            total[k, span, :] += both[:, 0:128] + both[:, 128:256] + third
            if part == 0:

                @pl.when(n % parts == parts - 1)
                def _():
                    for piece in range(SPLIT):
                        core_copy(k, piece).start()

        @pl.when(n == parts)
        def _():
            send_sums(0)

        return carry

    lax.fori_loop(0, M * parts, part_of, 0)

    send_sums(1)
    scale = L / jnp.sqrt(jnp.sum(responses[...], axis=0))
    take_sums(0)
    take_sums(1)

    take(injected.at[:, pl.ds(0, 4 * rows), :], inj_send.at[0])
    take(injected.at[:, pl.ds(0, 3 * rows), :], inj_send.at[1])
    take(responses.at[pl.ds(0, CHIPS - 1)], resp_send.at[0])
    for copy in pairs:
        copy.wait_send()
    for k in range(M):
        take(from_core.at[k], core_send.at[k])
        take(outgoing.at[k], sum_send.at[k])
    take(blocks.at[:, pl.ds(0, (N - 1) * rows), :], block_send.at[0])


def body(cycles, legendre, weight, filters, hits, flux, order):
    orders, rows, width = cycles.shape
    degrees = filters.shape[0]
    clusters = hits.shape[1]
    everyone = N * rows
    dma = pltpu.SemaphoreType.DMA
    anywhere = pl.BlockSpec(memory_space=pl.ANY)
    return pl.pallas_call(
        kernel,
        out_shape=pltpu.VMEM(cycles.shape, F32),
        in_specs=[anywhere] * 7,
        out_specs=pl.BlockSpec(memory_space=pltpu.VMEM),
        scratch_shapes=[
            pltpu.SMEM((orders,), jnp.int32),
            pltpu.VMEM((orders, rows, width), F32),
            pltpu.VMEM((1, rows), F32),
            pltpu.VMEM((S, F, degrees), F32),
            pltpu.VMEM((orders, clusters), jnp.int32),
            pltpu.VMEM((orders, clusters, width), F32),
            dma((6,)),
            pltpu.VMEM((orders, everyone, width), F32),
            pltpu.VMEM((orders, 2 * width, everyone), BF16),
            dma((2,)),
            dma((2,)),
            dma((2, 2)),
            pltpu.VMEM((N, orders, width), F32),
            dma((1,)),
            dma((1,)),
            pltpu.VMEM((orders, everyone, degrees), F32),
            dma((1,)),
            dma((len(PIECES),)),
            pltpu.VMEM((everyone, WIDE), BF16),
            pltpu.VMEM((everyone, WIDE), BF16),
            pltpu.VMEM((width, WIDE), F32),
            pltpu.VMEM((2 * width, WIDE), BF16),
            pltpu.VMEM((orders, everyone, width), F32),
            pltpu.VMEM((orders, everyone // 2, width), F32),
            dma((orders,)),
            dma((orders,)),
            pltpu.VMEM((orders, (CHIPS - 1) * rows, width), F32),
            pltpu.VMEM((orders, CHIPS - 1, rows, width), F32),
            pltpu.VMEM((orders, rows, width), F32),
            dma((orders,)),
            dma((orders,)),
        ],
        compiler_params=pltpu.CompilerParams(
            collective_id=0, has_side_effects=True, vmem_limit_bytes=60 * 1024 * 1024
        ),
    )(cycles, legendre, weight.reshape(1, rows), jnp.transpose(filters, (1, 2, 0)), hits, flux, order)


def solution(mesh):
    return jax.shard_map(
        body,
        mesh=mesh,
        in_specs=(
            P("order", "blk", None),
            P("order", "blk", None),
            P("blk"),
            P("blk", None, None),
            P("order", None),
            P("order", None, None),
            P("order"),
        ),
        out_specs=P("order", "blk", None),
        check_vma=False,
    )
```
